128 devices in a mesh: grp: 8 (over y, core), mem: 16 (over z, x).
Axes of the slice: x: 4, y: 4, z: 4, core: 2. Of those that a mesh axis runs over, the one named last changes fastest.
Arguments:
- coefficients: float32 [8, 240, 16384], P(None, None, ('grp', 'mem')), may hold values from -6 to 6
- incident: float32 [8, 240, 16384], P(None, None, ('grp', 'mem')), may hold values from -6 to 6
- mie_coeffs: float32 [2, 240], replicated, may hold values from -0.8 to 0.8
- rot_table: bfloat16 [8, 240, 240], replicated, may hold values from -0.375 to 0.375
- axial_shells: bfloat16 [3, 2, 240, 240], replicated, may hold values from -0.1875 to 0.1875
- up_axial: bfloat16 [2, 240, 240], replicated, may hold values from -0.1875 to 0.1875
- far_axial: bfloat16 [2, 240, 240], replicated, may hold values from -0.0625 to 0.0625
- coupling: float32 [256, 256], replicated, may hold values from 0.01 to 0.1
- cluster_ids: int32 [16384], P(('grp', 'mem')), may hold values from 0 to 31
- center_rot: int32 [16384], P(('grp', 'mem')), may hold values from 0 to 7
- pair_col: int32 [24, 16384], P(None, ('grp', 'mem')), may hold values from -1 to 1407, as said below
- pair_rot: int32 [24, 16384], P(None, ('grp', 'mem')), may hold values from -1 to 7, as said below
- send_col: int32 [768, 64], P(('grp', 'mem')), may hold values from 0 to 1023, as said below
Outputs:
- updated: float32 [8, 240, 16384], P(None, None, ('grp', 'mem'))
The draws below stay inside these ranges and needn't reach their ends.
Inputs may be any that keep to these rules, and one draw needn't show every extreme that they name: `pair_col`: -1 marks an empty slot; a value below 1024 is r * 128 + j for the own device's sphere j rotated by entry r; a larger one is 1024 + p * 64 + c for the c-th column sent to this device by its neighbour p; every such received column is named by some slot of the receiving device. `pair_rot`: -1 exactly in empty slots; otherwise the table entry with which the slot's column was rotated. `send_col`: row d * 6 + p lists the pool columns r * 128 + j that device d provides to the device whose neighbour p it is.
All inputs are finite; a program needn't handle non-finite values.
Results may differ from the reference program's by a relative error of at most 0.0038.
The reference program's roundings to bfloat16 on the way count: a program that leaves them out, or rounds other values in their place, can miss the bound.
Values may be sent and summed in bfloat16 or wider, within the bound.
No kernel may reach another device: no remote copies, remote signals or barrier semaphores. Data moves between devices by JAX's collectives and lax.ppermute only.
A program may use at most 128 MiB of HBM per device.

```python
import math
import jax
import jax.numpy as jnp
import numpy as np
from jax import lax

NCO = 240
NDIR = 4
NROT = 8
NSHELL = 3
SLOT = 8
NPEER = 6
SPH_DEV = 128
CAP = 64
NEAR = 24
NSPH = 16384
CL_GRP = 32
NCLUS = 256
N_GRP = 8
N_MEM = 16


def pair_tables(key):
    dev_count = NSPH // SPH_DEV
    pool_size = NROT * SPH_DEV
    recv_size = NPEER * CAP
    slot_count = NEAR * SPH_DEV
    base_key = jax.random.fold_in(key, 7013)
    sender = jax.random.randint(jax.random.fold_in(base_key, 1), (dev_count, NPEER, CAP), 0, pool_size, dtype=jnp.int32)
    dev_keys = jax.random.split(jax.random.fold_in(base_key, 2), dev_count)
    mem_steps = jnp.array([1, -1, 2, -2, 0, 0], dtype=jnp.int32)
    grp_steps = jnp.array([0, 0, 0, 0, 1, -1], dtype=jnp.int32)
    peer_iota = jnp.arange(NPEER, dtype=jnp.int32)

    def one_device(dev_key, target):
        grp_idx = target // N_MEM
        mem_idx = target % N_MEM
        sources = (grp_idx - grp_steps) % N_GRP * N_MEM + (mem_idx - mem_steps) % N_MEM
        ordering = jax.random.permutation(jax.random.fold_in(dev_key, 1), slot_count)
        ranking = jnp.argsort(ordering).astype(jnp.int32)
        alive = jax.random.randint(jax.random.fold_in(dev_key, 2), (slot_count,), 0, 2, dtype=jnp.int32)
        own_cols = jax.random.randint(jax.random.fold_in(dev_key, 3), (slot_count,), 0, pool_size, dtype=jnp.int32)
        incoming = sender[sources, peer_iota].reshape(-1)
        is_recv = ranking < recv_size
        rank_clip = jnp.minimum(ranking, recv_size - 1)
        col_vals = jnp.where(is_recv, pool_size + ranking, jnp.where(alive == 1, own_cols, -1))
        rot_vals = jnp.where(is_recv, incoming[rank_clip] // SPH_DEV, jnp.where(alive == 1, own_cols // SPH_DEV, -1))
        return (col_vals.reshape(NEAR, SPH_DEV), rot_vals.reshape(NEAR, SPH_DEV))
    col_table, rot_ints = jax.vmap(one_device)(dev_keys, jnp.arange(dev_count, dtype=jnp.int32))
    col_table = jnp.transpose(col_table, (1, 0, 2)).reshape(NEAR, NSPH).astype(jnp.int32)
    rot_ints = jnp.transpose(rot_ints, (1, 0, 2)).reshape(NEAR, NSPH).astype(jnp.int32)
    return (col_table, rot_ints, sender.reshape(dev_count * NPEER, CAP))


def draw_pair_col(key, part):
    return pair_tables(key)[0]


def draw_pair_rot(key, part):
    return pair_tables(key)[1]


def draw_send_col(key, part):
    return pair_tables(key)[2]


def plant(values, own_key, low, high):
    longest = values.shape.index(max(values.shape))
    spots = []
    for shift in (0, 1):
        where = [jax.random.randint(jax.random.fold_in(own_key, axis), (), 0, length) for axis, length in enumerate(values.shape)]
        where[longest] = (where[longest] + shift) % values.shape[longest]
        spots.append(tuple(where))
    return values.at[spots[0]].set(low).at[spots[1]].set(high)


def level_of(key, shape, cuts, low, largest):
    level = 1.0
    for axis_at, shards_of in cuts:
        heights = jax.random.uniform(jax.random.fold_in(jax.random.fold_in(key, 6), axis_at), (shards_of,), jnp.float32, low / len(cuts), largest / len(cuts))
        level = level * jnp.repeat(jnp.exp(heights), shape[axis_at] // shards_of).reshape((-1,) + (1,) * (len(shape) - 1 - axis_at))
    return level


def cumulative_ranks(count, lean):
    weights = [(1 << 20) // math.isqrt(rank ** lean) + 1 for rank in range(1, count + 1)]
    scale = 1 + sum(weights) // (1 << 30)
    return np.cumsum(np.array([max(1, weight // scale) for weight in weights]))


def ranked_ids(own_key, extent, count, skew):
    grid = cumulative_ranks(count, skew)
    ticket = jax.random.randint(jax.random.fold_in(own_key, 1), extent, 0, int(grid[count - 1]))
    grade = jnp.searchsorted(jnp.asarray(grid, jnp.int32), ticket, side="right")
    return jax.random.permutation(jax.random.fold_in(own_key, 2), count)[grade].astype(jnp.int32)


def centred(own_key, dims, deviation, limit, cuts=(), kind=jnp.bfloat16):
    result = deviation * jax.random.normal(own_key, dims, jnp.float32)
    if cuts:
        result = result * level_of(own_key, dims, cuts, -0.22, 0.18)
    return jnp.clip(result, -limit, limit).astype(kind)


def setup_inputs(seed: int = 0) -> dict:
    keys = jax.random.split(jax.random.key(seed), 14)
    return {
        "coefficients": centred(keys[0], (2 * NDIR, NCO, NSPH), 1.0, 6.0, ((2, 128),), jnp.float32),
        "incident": centred(keys[1], (2 * NDIR, NCO, NSPH), 1.0, 6.0, ((2, 128),), jnp.float32),
        "mie_coeffs": jnp.clip(jax.random.uniform(keys[2], (2, NCO), jnp.float32, -0.8, 0.8), -0.8, 0.8),
        "rot_table": centred(keys[3], (NROT, NCO, NCO), NCO ** -0.5, 0.375),
        "axial_shells": centred(keys[4], (NSHELL, 2, NCO, NCO), (4 * NCO) ** -0.5, 0.1875),
        "up_axial": centred(keys[5], (2, NCO, NCO), (4 * NCO) ** -0.5, 0.1875),
        "far_axial": centred(keys[6], (2, NCO, NCO), (40 * NCO) ** -0.5, 0.0625),
        "coupling": jnp.clip(jnp.exp(jax.random.uniform(keys[7], (NCLUS, NCLUS), jnp.float32, math.log(0.01), math.log(0.1))), 0.01, 0.1),
        "cluster_ids": plant(ranked_ids(keys[8], (NSPH,), CL_GRP, 2), jax.random.fold_in(keys[8], 3), 0, CL_GRP - 1).astype(jnp.int32),
        "center_rot": plant(jax.random.randint(keys[9], (NSPH,), 0, NROT), jax.random.fold_in(keys[9], 1), 0, NROT - 1).astype(jnp.int32),
        "pair_col": draw_pair_col(jax.random.fold_in(keys[13], 71), 0),
        "pair_rot": draw_pair_rot(jax.random.fold_in(keys[13], 71), 0),
        "send_col": draw_send_col(jax.random.fold_in(keys[13], 71), 0),
    }


def rounded(values):
    return lax.optimization_barrier(values.astype(jnp.bfloat16))


def complex_apply(matrix_pair, columns):
    dir_count = columns.shape[0] // 2
    real_in = columns[:dir_count].astype(jnp.float32)
    imag_in = columns[dir_count:].astype(jnp.float32)
    real_mat = matrix_pair[0].astype(jnp.float32)
    imag_mat = matrix_pair[1].astype(jnp.float32)
    real_out = jnp.einsum("kc,xcn->xkn", real_mat, real_in) - jnp.einsum("kc,xcn->xkn", imag_mat, imag_in)
    imag_out = jnp.einsum("kc,xcn->xkn", real_mat, imag_in) + jnp.einsum("kc,xcn->xkn", imag_mat, real_in)
    return jnp.concatenate([real_out, imag_out], axis=0)


def neighbour_sources(device):
    mem_steps = jnp.array([1, -1, 2, -2, 0, 0], dtype=jnp.int32)
    grp_steps = jnp.array([0, 0, 0, 0, 1, -1], dtype=jnp.int32)
    grp_idx = device // N_MEM
    mem_idx = device % N_MEM
    return (((grp_idx - grp_steps) % N_GRP) * N_MEM + (mem_idx - mem_steps) % N_MEM).astype(jnp.int32)


def reference(coefficients, incident, mie_coeffs, rot_table, axial_shells, up_axial, far_axial, coupling, cluster_ids, center_rot, pair_col, pair_rot, send_col):
    comps = coefficients.shape[0]
    dev_count = NSPH // SPH_DEV
    pool_size = NROT * SPH_DEV
    table_f = rot_table.astype(jnp.float32)
    highest = lax.Precision.HIGHEST

    def rotate_device(block):
        turned = jnp.einsum("rkc,xcn->xkrn", table_f, rounded(block).astype(jnp.float32))
        return rounded(turned).reshape(comps, NCO, pool_size)

    blocks = coefficients.reshape(comps, NCO, dev_count, SPH_DEV).transpose(2, 0, 1, 3)
    rotated = lax.map(rotate_device, blocks)
    pooled = rotated.transpose(1, 2, 0, 3).reshape(comps, NCO, dev_count * pool_size)
    sphere_ids = jnp.arange(NSPH, dtype=jnp.int32)
    owners = sphere_ids // SPH_DEV
    own_pick = owners * pool_size + center_rot * SPH_DEV + sphere_ids % SPH_DEV
    lifted = complex_apply(up_axial, jnp.take(pooled, own_pick, axis=2))
    global_cluster = (owners // N_MEM) * CL_GRP + cluster_ids
    cluster_iota = jnp.arange(NCLUS, dtype=jnp.int32)
    member_table = (global_cluster[:, None] == cluster_iota[None, :]).astype(jnp.float32)
    expansions = jnp.einsum("xkn,nc->xkc", lifted, member_table, precision=highest)
    off_diag = jnp.where(cluster_iota[:, None] == cluster_iota[None, :], jnp.float32(0.0), coupling)
    reached = jnp.einsum("cd,xkd->xkc", off_diag, expansions, precision=highest)
    far_cluster = complex_apply(far_axial, rounded(reached))
    far_each = jnp.take(far_cluster, global_cluster, axis=2)
    rot_iota = jnp.arange(NROT, dtype=jnp.int32)

    def device_field(device):
        first_sphere = device * SPH_DEV
        slot_cols = lax.dynamic_slice_in_dim(pair_col, first_sphere, SPH_DEV, 1)
        slot_rots = lax.dynamic_slice_in_dim(pair_rot, first_sphere, SPH_DEV, 1)
        own_rots = lax.dynamic_slice_in_dim(center_rot, first_sphere, SPH_DEV, 0)
        far_own = lax.dynamic_slice_in_dim(far_each, first_sphere, SPH_DEV, 2)
        sources = neighbour_sources(device)
        beyond = jnp.maximum(slot_cols - pool_size, 0)
        peer = jnp.minimum(beyond // CAP, NPEER - 1)
        source = sources[peer]
        sent_col = send_col[source * NPEER + peer, beyond % CAP]
        flat_index = jnp.where(slot_cols >= pool_size, source * pool_size + sent_col, device * pool_size + jnp.maximum(slot_cols, 0))
        fetched = jnp.take(pooled, flat_index.reshape(-1), axis=2)
        fetched = jnp.where((slot_cols >= 0).reshape(-1)[None, None, :], fetched, jnp.zeros((), fetched.dtype))
        shell_cols = fetched.reshape(comps, NCO, NSHELL, SLOT * SPH_DEV)
        pieces = []
        for shell_idx in range(NSHELL):
            pieces.append(complex_apply(axial_shells[shell_idx], shell_cols[:, :, shell_idx]))
        moved = jnp.stack(pieces, axis=2).reshape(comps, NCO, NEAR, SPH_DEV)
        selector = (slot_rots[:, None, :] == rot_iota[None, :, None]).astype(jnp.float32)
        own_select = (own_rots[None, :] == rot_iota[:, None]).astype(jnp.float32)
        totals = jnp.einsum("srn,xksn->rxkn", selector, moved, precision=highest) + own_select[:, None, None, :] * far_own[None]
        return jnp.einsum("rck,rxcn->xkn", table_f, rounded(totals).astype(jnp.float32))

    fields = lax.map(device_field, jnp.arange(dev_count, dtype=jnp.int32))
    field = fields.transpose(1, 2, 0, 3).reshape(comps, NCO, NSPH)
    summed = incident + field
    dir_count = comps // 2
    real_part = summed[:dir_count]
    imag_part = summed[dir_count:]
    mie_real = mie_coeffs[0][None, :, None]
    mie_imag = mie_coeffs[1][None, :, None]
    return jnp.concatenate([mie_real * real_part - mie_imag * imag_part, mie_real * imag_part + mie_imag * real_part], axis=0)
```

```python
import jax
import jax.numpy as jnp
from jax import lax
from jax.experimental import pallas as pl
from jax.experimental.pallas import tpu as pltpu
from jax.sharding import PartitionSpec as P

BF = jnp.bfloat16
F32 = jnp.float32
I32 = jnp.int32
VM = pl.BlockSpec(memory_space=pltpu.VMEM)


def nn_dot(a, b):
    return lax.dot_general(a, b, (((1,), (0,)), ((), ())), preferred_element_type=F32)


def iota(shape, dim):
    return lax.broadcasted_iota(I32, shape, dim)


def shifted(value, axis, by):
    length = lax.axis_size(axis)
    return lax.ppermute(value, axis, [(i, (i + by) % length) for i in range(length)])


def packed_complex(mat, cols):
    k = mat.shape[0] // 2
    both = nn_dot(mat, cols)
    sign = jnp.where(iota((k, 128), 1) < 64, -1.0, 1.0).astype(F32)
    return both[:k] + pltpu.roll(both[k:], 64, 1) * sign


def send_kernel(n_mem, coef, rot, send, crot, cid, up, pool, *rest):
    outs = rest[:6]
    far, xs, sel = rest[6:]
    n_x, n_k, n_i = coef.shape
    n_r = rot.shape[0]
    for x in range(n_x):
        xs[:, x * n_i : (x + 1) * n_i] = coef[x].astype(BF)
    x_all = xs[...]
    for r in range(n_r):
        turned = nn_dot(rot[r], x_all).astype(BF)
        for x in range(n_x):
            pool[x * n_k : (x + 1) * n_k, r * n_i : (r + 1) * n_i] = turned[
                :, x * n_i : (x + 1) * n_i
            ]
    rows = iota((n_r * n_i, 128), 0)
    for q in range(3):
        ids = jnp.concatenate([send[2 * q : 2 * q + 1, :], send[2 * q + 1 : 2 * q + 2, :]], axis=1)
        sel[:, q * 128 : (q + 1) * 128] = jnp.where(rows == ids, 1.0, 0.0).astype(BF)
    key = (crot[...] * 32 + cid[...]).astype(F32)
    key_t = jnp.transpose(jnp.broadcast_to(key, (n_i, n_i)))
    lanes = iota((n_i, n_i), 1)
    for r in range(n_r):
        hit = (key_t == (lanes + r * 32).astype(F32)) & (lanes < 32)
        sel[r * n_i : (r + 1) * n_i, 384:512] = jnp.where(hit, 1.0, 0.0).astype(BF)
    half = n_x // 2 * n_k
    real = nn_dot(pool[:half, :], sel[...])
    imag = nn_dot(pool[half:, :], sel[...])
    low = iota((half, 128), 1) < 64
    for q in range(3):
        re = real[:, q * 128 : (q + 1) * 128]
        im = imag[:, q * 128 : (q + 1) * 128]
        outs[2 * q][...] = jnp.where(low, re, pltpu.roll(im, 64, 1)).astype(BF)
        outs[2 * q + 1][...] = jnp.where(low, pltpu.roll(re, 64, 1), im).astype(BF)
    me = lax.axis_index("mem")
    chunk = 32
    far[lax.rem(2 * n_mem - 1 - me, n_mem)] = jnp.zeros((chunk, 128), F32)
    mat = up[...].reshape(2 * n_k, n_k)
    packed = []
    for xh in range(2):
        total = None
        for q in range(4):
            x = 2 * q + xh
            src = real if x < 4 else imag
            part = src[(x % 4) * n_k : (x % 4 + 1) * n_k, 384:512]
            part = pltpu.roll(part, 32 * q, 1) if q else part
            total = part if total is None else total + part
        hi = total.astype(BF)
        rem = total - hi.astype(F32)
        mid = rem.astype(BF)
        lo = (rem - mid.astype(F32)).astype(BF)
        packed.append(
            packed_complex(mat, lo) + packed_complex(mat, mid) + packed_complex(mat, hi)
        )
    whole = jnp.concatenate(packed, axis=0)
    for c in range(2 * n_k // chunk):
        far[lax.rem(n_mem + c - me, n_mem)] = whole[c * chunk : (c + 1) * chunk]


def own_kernel(pool, pcol, prot, axial, rot, g_out, sel_out, late_out, rt_out, mats, stack):
    r = pl.program_id(0)
    n_k = 240
    n_i = pcol.shape[1]

    @pl.when(r == 0)
    def _():
        mats[...] = jnp.zeros_like(mats)
        stack[...] = jnp.zeros_like(stack)
        for s in range(3):
            mats[:, s * 256 : s * 256 + n_k] = axial[s].reshape(2 * n_k, n_k)

    rt_out[...] = jnp.zeros_like(rt_out)
    rt_out[:, :n_k] = jnp.transpose(rot[0].astype(F32)).astype(BF)
    js = iota((n_i, n_i), 0)
    target = js + r * n_i
    counts = []
    for s in range(3):
        total = jnp.zeros((n_i, n_i), F32)
        for t in range(8):
            row = pcol[s * 8 + t : s * 8 + t + 1, :]
            total = total + jnp.where(row == target, 1.0, 0.0)
        counts.append(total.astype(BF))
    taken = nn_dot(pool[...], jnp.concatenate(counts, axis=1)).astype(BF)
    for s in range(3):
        for x in range(8):
            stack[s * 256 : s * 256 + n_k, x * n_i : (x + 1) * n_i] = taken[
                x * n_k : (x + 1) * n_k, s * n_i : (s + 1) * n_i
            ]
    both = nn_dot(mats[...], stack[...])
    half = 4 * n_i
    g_out[0, :, :half] = both[:n_k, :half] - both[n_k:, half:]
    g_out[0, :, half:] = both[n_k:, :half] + both[:n_k, half:]
    keys = jnp.where(pcol[...] >= 1024, pcol[...] - 1024 + prot[...] * 384, -1)
    for pb, pair in enumerate((0, 2, 1)):
        target = js + pair * 128 + r * 384
        for s in range(3):
            total = jnp.zeros((n_i, n_i), F32)
            for t in range(8):
                row = keys[s * 8 + t : s * 8 + t + 1, :]
                total = total + jnp.where(row == target, 1.0, 0.0)
            if pb < 2:
                at = (pb * 3 + s) * 128
                sel_out[at : at + 128, :] = total.astype(BF)
            else:
                late_out[s * 128 : (s + 1) * 128, :] = total.astype(BF)


def lift_pairs(pairs, axial, xs, moved):
    n_k = 240
    low = iota((n_k, 128), 1) < 64
    count = len(pairs)
    half = count * 512
    for j, (first, second) in enumerate(pairs):
        for d in range(4):
            a = first[d * n_k : (d + 1) * n_k, :].astype(F32)
            b = second[d * n_k : (d + 1) * n_k, :].astype(F32)
            at = (j * 4 + d) * 128
            xs[:, at : at + 128] = jnp.where(low, a, pltpu.roll(b, 64, 1)).astype(BF)
            xs[:, half + at : half + at + 128] = jnp.where(low, pltpu.roll(a, 64, 1), b).astype(BF)
    for s in range(3):
        both = nn_dot(axial[s].reshape(2 * n_k, n_k), xs[...])
        real = (both[:n_k, :half] - both[n_k:, half:]).astype(BF)
        imag = (both[n_k:, :half] + both[:n_k, half:]).astype(BF)
        for j in range(count):
            lane = (j * 3 + s) * 128
            for d in range(4):
                at = (j * 4 + d) * 128
                moved[d * n_k : (d + 1) * n_k, lane : lane + 128] = real[:, at : at + 128]
                moved[(4 + d) * n_k : (5 + d) * n_k, lane : lane + 128] = imag[:, at : at + 128]


def early_kernel(p0, p1, p4, p5, axial, sel, g_in, g_out, xs, moved):
    n_k = 240
    lift_pairs(((p0, p1), (p4, p5)), axial, xs, moved)
    for step in range(4):
        res = nn_dot(moved[...], sel[:, step * 256 : (step + 1) * 256])
        for rr in range(2):
            r = step * 2 + rr
            for x in range(8):
                g_out[r, :, x * 128 : (x + 1) * 128] = (
                    g_in[r, :, x * 128 : (x + 1) * 128]
                    + res[x * n_k : (x + 1) * n_k, rr * 128 : (rr + 1) * 128]
                )


def reach_kernel(blocks, coupling, out):
    me = lax.axis_index("grp")
    n_g = blocks.shape[0]
    rows = coupling[pl.ds(pl.multiple_of(me * 32, 32), 32), :]
    diag = iota((32, 256), 1) == iota((32, 256), 0) + me * 32
    rows = jnp.where(diag, 0.0, rows)
    lanes = iota((32, 128), 1)
    total = jnp.zeros((32, 128), F32)
    for gs in range(n_g):
        window = rows[:, gs // 4 * 128 : gs // 4 * 128 + 128]
        parts = []
        for q in range(4):
            by = (q * 32 - gs % 4 * 32) % 128
            moved = pltpu.roll(window, by, 1) if by else window
            parts.append(jnp.where((lanes >= q * 32) & (lanes < q * 32 + 32), moved, 0.0))
        mat = jnp.concatenate(parts, axis=0)
        block = blocks[lax.rem(n_g + me - gs, n_g)]
        total = total + lax.dot_general(
            block,
            mat,
            (((1,), (1,)), ((), ())),
            preferred_element_type=F32,
            precision=lax.Precision.HIGHEST,
        )
    out[...] = total.astype(BF)


def final_kernel(
    p2, p3, axial, sel, g_in, far_in, far_axial, cid, crot, rt, incident, mie, out,
    xs, moved, gb, fin, fsum
):
    n_k = 240
    n_mem = far_in.shape[0]
    lift_pairs(((p2, p3),), axial, xs, moved)
    me = lax.axis_index("mem")
    for c in range(n_mem):
        fin[c * 32 : (c + 1) * 32, :] = far_in[lax.rem(n_mem + me - c, n_mem)]
    mat = far_axial[...].reshape(2 * n_k, n_k)
    ids = jnp.broadcast_to(cid[...], (n_k, 128))
    for xh in range(2):
        cluster = packed_complex(mat, fin[xh * n_k : (xh + 1) * n_k, :])
        for q in range(4):
            fsum[2 * q + xh] = jnp.take_along_axis(cluster, ids + q * 32, axis=1)
    turn = jnp.broadcast_to(crot[...], (n_k, 128))
    pad = jnp.zeros((16, 1024), BF)
    for step in range(4):
        res = nn_dot(moved[...], sel[:, step * 256 : (step + 1) * 256])
        for rr in range(2):
            r = step * 2 + rr
            mine = turn == r
            for x in range(8):
                total = (
                    g_in[r, :, x * 128 : (x + 1) * 128]
                    + res[x * n_k : (x + 1) * n_k, rr * 128 : (rr + 1) * 128]
                    + jnp.where(mine, fsum[x], 0.0)
                )
                gb[r * 256 : r * 256 + n_k, x * 128 : (x + 1) * 128] = total.astype(BF)
            gb[r * 256 + n_k : (r + 1) * 256, :] = pad
    field = nn_dot(rt[...], gb[...])
    mie_re = jnp.transpose(jnp.broadcast_to(mie[0:1, :], (128, n_k)))
    mie_im = jnp.transpose(jnp.broadcast_to(mie[1:2, :], (128, n_k)))
    for d in range(4):
        re = incident[d] + field[:, d * 128 : (d + 1) * 128]
        im = incident[4 + d] + field[:, (4 + d) * 128 : (5 + d) * 128]
        out[d] = mie_re * re - mie_im * im
        out[4 + d] = mie_re * im + mie_im * re


def params(mib):
    return pltpu.CompilerParams(vmem_limit_bytes=mib << 20)


def on_device(
    coefficients,
    incident,
    mie_coeffs,
    rot_table,
    axial_shells,
    up_axial,
    far_axial,
    coupling,
    cluster_ids,
    center_rot,
    pair_col,
    pair_rot,
    send_col,
):
    sds = jax.ShapeDtypeStruct
    n_mem = lax.axis_size("mem")
    cid = cluster_ids.reshape(1, 128)
    crot = center_rot.reshape(1, 128)
    first = pl.pallas_call(
        lambda *refs: send_kernel(n_mem, *refs),
        out_shape=[sds((1920, 1024), BF)] + [sds((960, 128), BF)] * 6 + [sds((n_mem, 32, 128), F32)],
        in_specs=[VM] * 6,
        out_specs=[VM] * 8,
        scratch_shapes=[pltpu.VMEM((240, 1024), BF), pltpu.VMEM((1024, 512), BF)],
        compiler_params=params(40),
        name="send",
    )(coefficients, rot_table, send_col, crot, cid, up_axial)
    pool = first[0]
    sends = first[1:7]
    acc = first[7]
    moves = (("mem", 1), ("mem", -1), ("mem", 2), ("mem", -2), ("grp", 1), ("grp", -1))
    got = [None] * 6
    for p in (2, 3, 0, 1, 4, 5):
        got[p] = shifted(sends[p], *moves[p])
    size = n_mem // 2
    while size:
        acc = acc[:size] + shifted(acc[size:], "mem", size)
        size //= 2
    step = 1
    while step < lax.axis_size("grp"):
        acc = jnp.concatenate([acc, shifted(acc, "grp", step)], axis=0)
        step *= 2
    reached = pl.pallas_call(
        reach_kernel,
        out_shape=sds((32, 128), BF),
        in_specs=[VM] * 2,
        out_specs=VM,
        name="reach",
    )(acc, coupling)[None]
    step = 1
    while step < n_mem:
        reached = jnp.concatenate([reached, shifted(reached, "mem", step)], axis=0)
        step *= 2
    g_own, sel, sel_late, rt = pl.pallas_call(
        own_kernel,
        grid=(8,),
        out_shape=[sds((8, 240, 1024), F32), sds((768, 1024), BF), sds((384, 1024), BF), sds((240, 2048), BF)],
        in_specs=[
            pl.BlockSpec((1920, 128), lambda r: (0, r)),
            pl.BlockSpec((24, 128), lambda r: (0, 0)),
            pl.BlockSpec((24, 128), lambda r: (0, 0)),
            pl.BlockSpec((3, 2, 240, 240), lambda r: (0, 0, 0, 0)),
            pl.BlockSpec((1, 240, 240), lambda r: (r, 0, 0)),
        ],
        out_specs=[
            pl.BlockSpec((1, 240, 1024), lambda r: (r, 0, 0)),
            pl.BlockSpec((768, 128), lambda r: (0, r)),
            pl.BlockSpec((384, 128), lambda r: (0, r)),
            pl.BlockSpec((240, 256), lambda r: (0, r)),
        ],
        scratch_shapes=[pltpu.VMEM((480, 768), BF), pltpu.VMEM((768, 1024), BF)],
        compiler_params=params(40),
        name="own",
    )(pool, pair_col, pair_rot, axial_shells, rot_table)
    g_early = pl.pallas_call(
        early_kernel,
        out_shape=sds((8, 240, 1024), F32),
        in_specs=[VM] * 7,
        out_specs=VM,
        scratch_shapes=[pltpu.VMEM((240, 2048), BF), pltpu.VMEM((1920, 768), BF)],
        compiler_params=params(48),
        name="early",
    )(got[0], got[1], got[4], got[5], axial_shells, sel, g_own)
    return pl.pallas_call(
        final_kernel,
        out_shape=sds((8, 240, 128), F32),
        in_specs=[VM] * 12,
        out_specs=VM,
        scratch_shapes=[
            pltpu.VMEM((240, 1024), BF),
            pltpu.VMEM((1920, 384), BF),
            pltpu.VMEM((2048, 1024), BF),
            pltpu.VMEM((512, 128), BF),
            pltpu.VMEM((8, 240, 128), F32),
        ],
        compiler_params=params(48),
        name="final",
    )(
        got[2], got[3], axial_shells, sel_late, g_early, reached, far_axial, cid, crot, rt,
        incident, mie_coeffs,
    )


def solution(mesh):
    in_specs = (
        P(None, None, ("grp", "mem")),
        P(None, None, ("grp", "mem")),
        P(),
        P(),
        P(),
        P(),
        P(),
        P(),
        P(("grp", "mem")),
        P(("grp", "mem")),
        P(None, ("grp", "mem")),
        P(None, ("grp", "mem")),
        P(("grp", "mem"), None),
    )
    out_specs = P(None, None, ("grp", "mem"))
    return jax.shard_map(
        on_device, mesh=mesh, in_specs=in_specs, out_specs=out_specs, check_vma=False
    )
```

```python
import jax
import jax.numpy as jnp
from jax import lax
from jax.experimental import pallas as pl
from jax.experimental.pallas import tpu as pltpu
from jax.sharding import PartitionSpec as P


BF = jnp.bfloat16
F32 = jnp.float32
I32 = jnp.int32
VM = pl.BlockSpec(memory_space=pltpu.VMEM)


def nn_dot(a, b):
    return lax.dot_general(a, b, (((1,), (0,)), ((), ())), preferred_element_type=F32)


def iota(shape, dim):
    return lax.broadcasted_iota(I32, shape, dim)


def shifted(value, axis, by):
    length = lax.axis_size(axis)
    return lax.ppermute(value, axis, [(i, (i + by) % length) for i in range(length)])


def packed_complex(mat, cols):
    k = mat.shape[0] // 2
    both = nn_dot(mat, cols)
    sign = jnp.where(iota((k, 128), 1) < 64, -1.0, 1.0).astype(F32)
    return both[:k] + pltpu.roll(both[k:], 64, 1) * sign


def send_kernel(n_mem, coef_h, rot_h, send_h, crot_h, cid_h, up_h, *rest):
    pools = rest[:8]
    outs = rest[8:14]
    far, coef, rot, send, crot, cid, up, xs, sel, sems = rest[14:]
    pairs = ((coef_h, coef), (rot_h, rot), (send_h, send), (crot_h, crot), (cid_h, cid), (up_h, up))
    copies = [pltpu.make_async_copy(src, dst, sems.at[i]) for i, (src, dst) in enumerate(pairs)]
    for copy in copies:
        copy.start()
    n_x, n_k, n_i = coef.shape
    n_r = rot.shape[0]
    for i in (2, 3, 4):
        copies[i].wait()
    rows = iota((n_r * n_i, 128), 0)
    for q in range(3):
        ids = jnp.concatenate([send[2 * q : 2 * q + 1, :], send[2 * q + 1 : 2 * q + 2, :]], axis=1)
        sel[:, q * 128 : (q + 1) * 128] = jnp.where(rows == ids, 1.0, 0.0).astype(BF)
    key = (crot[...] * 32 + cid[...]).astype(F32)
    key_t = jnp.transpose(jnp.broadcast_to(key, (n_i, n_i)))
    lanes = iota((n_i, n_i), 1)
    for r in range(n_r):
        hit = (key_t == (lanes + r * 32).astype(F32)) & (lanes < 32)
        sel[r * n_i : (r + 1) * n_i, 384:512] = jnp.where(hit, 1.0, 0.0).astype(BF)
    for i in (0, 1, 5):
        copies[i].wait()
    for x in range(n_x):
        xs[:, x * n_i : (x + 1) * n_i] = coef[x].astype(BF)
    x_all = xs[...]
    for r in range(n_r):
        turned = nn_dot(rot[r], x_all).astype(BF)
        for x in range(n_x):
            pools[r][x * n_k : (x + 1) * n_k, :] = turned[:, x * n_i : (x + 1) * n_i]
    half = n_x // 2 * n_k
    real = nn_dot(jnp.concatenate([p[:half, :] for p in pools], axis=1), sel[...])
    imag = nn_dot(jnp.concatenate([p[half:, :] for p in pools], axis=1), sel[...])
    low = iota((half, 128), 1) < 64
    for q in range(3):
        re = real[:, q * 128 : (q + 1) * 128]
        im = imag[:, q * 128 : (q + 1) * 128]
        outs[2 * q][...] = jnp.where(low, re, pltpu.roll(im, 64, 1)).astype(BF)
        outs[2 * q + 1][...] = jnp.where(low, pltpu.roll(re, 64, 1), im).astype(BF)
    me = lax.axis_index("mem")
    chunk = 32
    far[lax.rem(2 * n_mem - 1 - me, n_mem)] = jnp.zeros((chunk, 128), F32)
    mat = up[...].reshape(2 * n_k, n_k)
    packed = []
    for xh in range(2):
        total = None
        for q in range(4):
            x = 2 * q + xh
            src = real if x < 4 else imag
            part = src[(x % 4) * n_k : (x % 4 + 1) * n_k, 384:512]
            part = pltpu.roll(part, 32 * q, 1) if q else part
            total = part if total is None else total + part
        hi = total.astype(BF)
        rem = total - hi.astype(F32)
        mid = rem.astype(BF)
        lo = (rem - mid.astype(F32)).astype(BF)
        packed.append(
            packed_complex(mat, lo) + packed_complex(mat, mid) + packed_complex(mat, hi)
        )
    whole = jnp.concatenate(packed, axis=0)
    for c in range(2 * n_k // chunk):
        far[lax.rem(n_mem + c - me, n_mem)] = whole[c * chunk : (c + 1) * chunk]


def own_kernel(r, *refs):
    if r == 0:
        pool, pcol, prot, rot, axial, g_out, sel_out, rt_out, mats, stack = refs
    else:
        pool, pcol, prot, rot, mats, g_out, sel_out, rt_out, stack = refs
    n_k = 240
    n_i = pcol.shape[1]
    if r == 0:
        mats[...] = jnp.zeros_like(mats)
        for s in range(3):
            mats[:, s * 256 : s * 256 + n_k] = axial[s].reshape(2 * n_k, n_k)
    for s in range(3):
        stack[s * 256 + n_k : (s + 1) * 256, :] = jnp.zeros((16, 8 * n_i), BF)
    rt_out[...] = jnp.zeros_like(rt_out)
    rt_out[:, :n_k] = jnp.transpose(rot[r].astype(F32)).astype(BF)
    js = iota((n_i, n_i), 0)
    counts = []
    for s in range(3):
        total = jnp.zeros((n_i, n_i), F32)
        for t in range(8):
            row = pcol[s * 8 + t : s * 8 + t + 1, :]
            total = total + jnp.where(row == js + r * n_i, 1.0, 0.0)
        counts.append(total.astype(BF))
    taken = nn_dot(pool[...], jnp.concatenate(counts, axis=1)).astype(BF)
    for s in range(3):
        for x in range(8):
            stack[s * 256 : s * 256 + n_k, x * n_i : (x + 1) * n_i] = taken[
                x * n_k : (x + 1) * n_k, s * n_i : (s + 1) * n_i
            ]
    both = nn_dot(mats[...], stack[...])
    half = 4 * n_i
    g_out[:, :half] = both[:n_k, :half] - both[n_k:, half:]
    g_out[:, half:] = both[n_k:, :half] + both[:n_k, half:]
    keys = jnp.where(pcol[...] >= 1024, pcol[...] - 1024 + prot[...] * 384, -1)
    for pair in range(3):
        for s in range(3):
            total = jnp.zeros((n_i, n_i), F32)
            for t in range(8):
                row = keys[s * 8 + t : s * 8 + t + 1, :]
                total = total + jnp.where(row == js + pair * 128 + r * 384, 1.0, 0.0)
            at = (pair * 3 + s) * 128
            sel_out[at : at + 128, :] = total.astype(BF)


def lift_kernel(first, second, axial, moved, xs):
    n_k = 240
    low = iota((n_k, 128), 1) < 64
    for d in range(4):
        a = first[d * n_k : (d + 1) * n_k, :].astype(F32)
        b = second[d * n_k : (d + 1) * n_k, :].astype(F32)
        at = d * 128
        xs[:, at : at + 128] = jnp.where(low, a, pltpu.roll(b, 64, 1)).astype(BF)
        xs[:, 512 + at : 512 + at + 128] = jnp.where(low, pltpu.roll(a, 64, 1), b).astype(BF)
    for s in range(3):
        both = nn_dot(axial[s].reshape(2 * n_k, n_k), xs[...])
        real = (both[:n_k, :512] - both[n_k:, 512:]).astype(BF)
        imag = (both[n_k:, :512] + both[:n_k, 512:]).astype(BF)
        lane = s * 128
        for d in range(4):
            at = d * 128
            moved[d * n_k : (d + 1) * n_k, lane : lane + 128] = real[:, at : at + 128]
            moved[(4 + d) * n_k : (5 + d) * n_k, lane : lane + 128] = imag[:, at : at + 128]


def recv_kernel(m0, m1, m2, sel_a, sel_b, g_a, g_b, g_out):
    n_k = 240
    moved = jnp.concatenate([m0[...], m1[...], m2[...]], axis=1)
    res = nn_dot(moved, jnp.concatenate([sel_a[...], sel_b[...]], axis=1))
    for rr, g_in in enumerate((g_a, g_b)):
        for x in range(8):
            g_out[rr, :, x * 128 : (x + 1) * 128] = (
                g_in[:, x * 128 : (x + 1) * 128]
                + res[x * n_k : (x + 1) * n_k, rr * 128 : (rr + 1) * 128]
            )


def reach_kernel(blocks, coupling, out):
    me = lax.axis_index("grp")
    n_g = blocks.shape[0]
    rows = coupling[pl.ds(pl.multiple_of(me * 32, 32), 32), :]
    diag = iota((32, 256), 1) == iota((32, 256), 0) + me * 32
    rows = jnp.where(diag, 0.0, rows)
    lanes = iota((32, 128), 1)
    total = jnp.zeros((32, 128), F32)
    for gs in range(n_g):
        window = rows[:, gs // 4 * 128 : gs // 4 * 128 + 128]
        parts = []
        for q in range(4):
            by = (q * 32 - gs % 4 * 32) % 128
            moved = pltpu.roll(window, by, 1) if by else window
            parts.append(jnp.where((lanes >= q * 32) & (lanes < q * 32 + 32), moved, 0.0))
        mat = jnp.concatenate(parts, axis=0)
        block = blocks[lax.rem(n_g + me - gs, n_g)]
        total = total + lax.dot_general(
            block,
            mat,
            (((1,), (1,)), ((), ())),
            preferred_element_type=F32,
            precision=lax.Precision.HIGHEST,
        )
    out[...] = total.astype(BF)


def final_kernel(*refs):
    gs = refs[:4]
    rts = refs[4:12]
    far_in, far_axial, cid, crot, incident, mie, out, gb, fin, fsum = refs[12:]
    n_k = 240
    n_mem = far_in.shape[0]
    me = lax.axis_index("mem")
    for c in range(n_mem):
        fin[c * 32 : (c + 1) * 32, :] = far_in[lax.rem(n_mem + me - c, n_mem)]
    mat = far_axial[...].reshape(2 * n_k, n_k)
    ids = jnp.broadcast_to(cid[...], (n_k, 128))
    for xh in range(2):
        cluster = packed_complex(mat, fin[xh * n_k : (xh + 1) * n_k, :])
        for q in range(4):
            fsum[2 * q + xh] = jnp.take_along_axis(cluster, ids + q * 32, axis=1)
    turn = jnp.broadcast_to(crot[...], (n_k, 128))
    pad = jnp.zeros((16, 1024), BF)
    for r in range(8):
        mine = turn == r
        for x in range(8):
            total = gs[r // 2][r % 2, :, x * 128 : (x + 1) * 128] + jnp.where(mine, fsum[x], 0.0)
            gb[r * 256 : r * 256 + n_k, x * 128 : (x + 1) * 128] = total.astype(BF)
        gb[r * 256 + n_k : (r + 1) * 256, :] = pad
    field = nn_dot(jnp.concatenate([t[...] for t in rts], axis=1), gb[...])
    mie_re = jnp.transpose(jnp.broadcast_to(mie[0:1, :], (128, n_k)))
    mie_im = jnp.transpose(jnp.broadcast_to(mie[1:2, :], (128, n_k)))
    for d in range(4):
        re = incident[d] + field[:, d * 128 : (d + 1) * 128]
        im = incident[4 + d] + field[:, (4 + d) * 128 : (5 + d) * 128]
        out[d] = mie_re * re - mie_im * im
        out[4 + d] = mie_re * im + mie_im * re


def params(mib):
    return pltpu.CompilerParams(vmem_limit_bytes=mib << 20)


def cost(flops, bytes_accessed):
    return pl.CostEstimate(flops=int(flops), transcendentals=0, bytes_accessed=int(bytes_accessed))


def on_device(
    coefficients,
    incident,
    mie_coeffs,
    rot_table,
    axial_shells,
    up_axial,
    far_axial,
    coupling,
    cluster_ids,
    center_rot,
    pair_col,
    pair_rot,
    send_col,
):
    sds = jax.ShapeDtypeStruct
    n_mem = lax.axis_size("mem")
    cid = cluster_ids.reshape(1, 128)
    crot = center_rot.reshape(1, 128)
    first = pl.pallas_call(
        lambda *refs: send_kernel(n_mem, *refs),
        out_shape=[sds((1920, 128), BF)] * 8 + [sds((960, 128), BF)] * 6 + [sds((n_mem, 32, 128), F32)],
        in_specs=[pl.BlockSpec(memory_space=pltpu.MemorySpace.HBM)] * 6,
        out_specs=[VM] * 15,
        scratch_shapes=[
            pltpu.VMEM((8, 240, 128), F32),
            pltpu.VMEM((8, 240, 240), BF),
            pltpu.VMEM((6, 64), I32),
            pltpu.VMEM((1, 128), I32),
            pltpu.VMEM((1, 128), I32),
            pltpu.VMEM((2, 240, 240), BF),
            pltpu.VMEM((240, 1024), BF),
            pltpu.VMEM((1024, 512), BF),
            pltpu.SemaphoreType.DMA((6,)),
        ],
        compiler_params=params(24),
        name="send",
    )(*[pltpu.with_memory_space_constraint(v, pltpu.HBM) for v in (coefficients, rot_table, send_col, crot, cid, up_axial)])
    pools = first[:8]
    sends = first[8:14]
    acc = first[14]
    moves = (("mem", 1), ("mem", -1), ("mem", 2), ("mem", -2), ("grp", 1), ("grp", -1))
    got = []
    for p in range(6):
        got.append(shifted(sends[p], *moves[p]))
    size = n_mem // 2
    while size:
        come = shifted(acc[size:], "mem", size)
        acc = acc[:size] + come
        size //= 2
    step = 1
    while step < lax.axis_size("grp"):
        come = shifted(acc, "grp", step)
        acc = jnp.concatenate([acc, come], axis=0)
        step *= 2
    reached = pl.pallas_call(
        reach_kernel,
        out_shape=sds((32, 128), BF),
        in_specs=[VM] * 2,
        out_specs=VM,
        compiler_params=params(2),
        name="reach",
    )(acc, coupling)[None]
    step = 1
    while step < n_mem:
        come = shifted(reached, "mem", step)
        reached = jnp.concatenate([reached, come], axis=0)
        step *= 2
    g_own, sels, rts = [], [], []
    mats = None
    for r in range(8):
        res = pl.pallas_call(
            lambda *refs, r=r: own_kernel(r, *refs),
            out_shape=[sds((240, 1024), F32), sds((1152, 128), BF), sds((240, 256), BF)]
            + ([sds((480, 768), BF)] if r == 0 else []),
            in_specs=[VM] * 5,
            out_specs=[VM] * (4 if r == 0 else 3),
            scratch_shapes=[pltpu.VMEM((768, 1024), BF)],
            compiler_params=params(20),
            cost_estimate=cost(1.26e9, 3e6),
        )(pools[r], pair_col, pair_rot, rot_table, axial_shells if r == 0 else mats)
        if r == 0:
            mats = res[3]
        g_own.append(res[0])
        sels.append(res[1])
        rts.append(res[2])
    lifted = []
    for j in range(3):
        lifted.append(
            pl.pallas_call(
                lift_kernel,
                out_shape=sds((1920, 384), BF),
                in_specs=[VM] * 3,
                out_specs=VM,
                scratch_shapes=[pltpu.VMEM((240, 1024), BF)],
                compiler_params=params(20),
                cost_estimate=cost(0.7e9, 3e6),
            )(got[2 * j], got[2 * j + 1], axial_shells)
        )
    totals = []
    for q in range(4):
        totals.append(
            pl.pallas_call(
                recv_kernel,
                out_shape=sds((2, 240, 1024), F32),
                in_specs=[VM] * 7,
                out_specs=VM,
                compiler_params=params(20),
                cost_estimate=cost(1.2e9, 8e6),
            )(*lifted, sels[2 * q], sels[2 * q + 1], g_own[2 * q], g_own[2 * q + 1])
        )
    return pl.pallas_call(
        final_kernel,
        out_shape=sds((8, 240, 128), F32),
        in_specs=[VM] * 18,
        out_specs=VM,
        scratch_shapes=[
            pltpu.VMEM((2048, 1024), BF),
            pltpu.VMEM((512, 128), BF),
            pltpu.VMEM((8, 240, 128), F32),
        ],
        compiler_params=params(20),
        name="final",
    )(*totals, *rts, reached, far_axial, cid, crot, incident, mie_coeffs)


def solution(mesh):
    in_specs = (
        P(None, None, ("grp", "mem")),
        P(None, None, ("grp", "mem")),
        P(),
        P(),
        P(),
        P(),
        P(),
        P(),
        P(("grp", "mem")),
        P(("grp", "mem")),
        P(None, ("grp", "mem")),
        P(None, ("grp", "mem")),
        P(("grp", "mem"), None),
    )
    out_specs = P(None, None, ("grp", "mem"))

    return jax.shard_map(
        on_device, mesh=mesh, in_specs=in_specs, out_specs=out_specs, check_vma=False
    )
```

```python
import jax
import jax.numpy as jnp
from jax import lax
from jax.experimental import pallas as pl
from jax.experimental.pallas import tpu as pltpu
from jax.sharding import PartitionSpec as P


BF = jnp.bfloat16
F32 = jnp.float32
I32 = jnp.int32
VM = pl.BlockSpec(memory_space=pltpu.VMEM)


def nn_dot(a, b):
    return lax.dot_general(a, b, (((1,), (0,)), ((), ())), preferred_element_type=F32)


def iota(shape, dim):
    return lax.broadcasted_iota(I32, shape, dim)


def moved_by(value, axis, target):
    length = lax.axis_size(axis)
    return lax.ppermute(value, axis, [(i, target(i)) for i in range(length)])


def shifted(value, axis, by):
    length = lax.axis_size(axis)
    return moved_by(value, axis, lambda i: (i + by) % length)


def packed_complex(mat, cols):
    k = mat.shape[0] // 2
    both = nn_dot(mat, cols)
    sign = jnp.where(iota((k, 128), 1) < 64, -1.0, 1.0).astype(F32)
    return both[:k] + pltpu.roll(both[k:], 64, 1) * sign


def send_kernel(coef_h, rot_h, send_h, crot_h, cid_h, up_h, *rest):
    pools = rest[:8]
    outs = rest[8:14]
    fars = rest[14:18]
    coef, rot, send, crot, cid, up, xs, sel, whole, sems = rest[18:]
    pairs = ((coef_h, coef), (rot_h, rot), (send_h, send), (crot_h, crot), (cid_h, cid), (up_h, up))
    copies = [pltpu.make_async_copy(src, dst, sems.at[i]) for i, (src, dst) in enumerate(pairs)]
    for copy in copies:
        copy.start()
    n_x, n_k, n_i = coef.shape
    n_r = rot.shape[0]
    for i in (2, 3, 4):
        copies[i].wait()
    rows = iota((n_r * n_i, 128), 0)
    for q in range(3):
        ids = jnp.concatenate([send[2 * q : 2 * q + 1, :], send[2 * q + 1 : 2 * q + 2, :]], axis=1)
        sel[:, q * 128 : (q + 1) * 128] = jnp.where(rows == ids, 1.0, 0.0).astype(BF)
    key = (crot[...] * 32 + cid[...]).astype(F32)
    key_t = jnp.transpose(jnp.broadcast_to(key, (n_i, n_i)))
    lanes = iota((n_i, n_i), 1)
    for r in range(n_r):
        hit = (key_t == (lanes + r * 32).astype(F32)) & (lanes < 32)
        sel[r * n_i : (r + 1) * n_i, 384:512] = jnp.where(hit, 1.0, 0.0).astype(BF)
    for i in (0, 1, 5):
        copies[i].wait()
    for x in range(n_x):
        xs[:, x * n_i : (x + 1) * n_i] = coef[x].astype(BF)
    x_all = xs[...]
    for r in range(n_r):
        turned = nn_dot(rot[r], x_all).astype(BF)
        for x in range(n_x):
            pools[r][x * n_k : (x + 1) * n_k, :] = turned[:, x * n_i : (x + 1) * n_i]
    half = n_x // 2 * n_k
    real = nn_dot(jnp.concatenate([p[:half, :] for p in pools], axis=1), sel[...])
    imag = nn_dot(jnp.concatenate([p[half:, :] for p in pools], axis=1), sel[...])
    low = iota((half, 128), 1) < 64
    for q in range(3):
        re = real[:, q * 128 : (q + 1) * 128]
        im = imag[:, q * 128 : (q + 1) * 128]
        outs[2 * q][...] = jnp.where(low, re, pltpu.roll(im, 64, 1)).astype(BF)
        outs[2 * q + 1][...] = jnp.where(low, pltpu.roll(re, 64, 1), im).astype(BF)
    mat = up[...].reshape(2 * n_k, n_k)
    for xh in range(2):
        total = None
        for q in range(4):
            x = 2 * q + xh
            src = real if x < 4 else imag
            part = src[(x % 4) * n_k : (x % 4 + 1) * n_k, 384:512]
            part = pltpu.roll(part, 32 * q, 1) if q else part
            total = part if total is None else total + part
        hi = total.astype(BF)
        rem = total - hi.astype(F32)
        mid = rem.astype(BF)
        lo = (rem - mid.astype(F32)).astype(BF)
        whole[xh * n_k : (xh + 1) * n_k, :] = (
            packed_complex(mat, lo) + packed_complex(mat, mid) + packed_complex(mat, hi)
        )
    whole[2 * n_k :, :] = jnp.zeros((512 - 2 * n_k, 128), F32)
    z = lax.axis_index("mem") // 4
    for k in range(4):
        at = pl.multiple_of(lax.rem(z + k, 4) * 128, 128)
        fars[k][...] = whole[pl.ds(at, 128), :]


def own_kernel(r, *refs):
    if r == 0:
        pool, pcol, prot, rot, axial, g_out, sel_out, rt_out, mats, stack = refs
    else:
        pool, pcol, prot, rot, mats, g_out, sel_out, rt_out, stack = refs
    n_k = 240
    n_i = pcol.shape[1]
    if r == 0:
        mats[...] = jnp.zeros_like(mats)
        for s in range(3):
            mats[:, s * 256 : s * 256 + n_k] = axial[s].reshape(2 * n_k, n_k)
    for s in range(3):
        stack[s * 256 + n_k : (s + 1) * 256, :] = jnp.zeros((16, 8 * n_i), BF)
    rt_out[...] = jnp.zeros_like(rt_out)
    rt_out[:, :n_k] = jnp.transpose(rot[r].astype(F32)).astype(BF)
    js = iota((n_i, n_i), 0)
    counts = []
    for s in range(3):
        total = jnp.zeros((n_i, n_i), F32)
        for t in range(8):
            row = pcol[s * 8 + t : s * 8 + t + 1, :]
            total = total + jnp.where(row == js + r * n_i, 1.0, 0.0)
        counts.append(total.astype(BF))
    taken = nn_dot(pool[...], jnp.concatenate(counts, axis=1)).astype(BF)
    for s in range(3):
        for x in range(8):
            stack[s * 256 : s * 256 + n_k, x * n_i : (x + 1) * n_i] = taken[
                x * n_k : (x + 1) * n_k, s * n_i : (s + 1) * n_i
            ]
    both = nn_dot(mats[...], stack[...])
    half = 4 * n_i
    g_out[:, :half] = both[:n_k, :half] - both[n_k:, half:]
    g_out[:, half:] = both[n_k:, :half] + both[:n_k, half:]
    keys = jnp.where(pcol[...] >= 1024, pcol[...] - 1024 + prot[...] * 384, -1)
    for pair in range(3):
        for s in range(3):
            total = jnp.zeros((n_i, n_i), F32)
            for t in range(8):
                row = keys[s * 8 + t : s * 8 + t + 1, :]
                total = total + jnp.where(row == js + pair * 128 + r * 384, 1.0, 0.0)
            at = (pair * 3 + s) * 128
            sel_out[at : at + 128, :] = total.astype(BF)


def lift_kernel(first, second, axial, moved, xs):
    n_k = 240
    low = iota((n_k, 128), 1) < 64
    for d in range(4):
        a = first[d * n_k : (d + 1) * n_k, :].astype(F32)
        b = second[d * n_k : (d + 1) * n_k, :].astype(F32)
        at = d * 128
        xs[:, at : at + 128] = jnp.where(low, a, pltpu.roll(b, 64, 1)).astype(BF)
        xs[:, 512 + at : 512 + at + 128] = jnp.where(low, pltpu.roll(a, 64, 1), b).astype(BF)
    for s in range(3):
        both = nn_dot(axial[s].reshape(2 * n_k, n_k), xs[...])
        real = (both[:n_k, :512] - both[n_k:, 512:]).astype(BF)
        imag = (both[n_k:, :512] + both[:n_k, 512:]).astype(BF)
        lane = s * 128
        for d in range(4):
            at = d * 128
            moved[d * n_k : (d + 1) * n_k, lane : lane + 128] = real[:, at : at + 128]
            moved[(4 + d) * n_k : (5 + d) * n_k, lane : lane + 128] = imag[:, at : at + 128]


def recv_kernel(m0, m1, m2, sel_a, sel_b, g_a, g_b, g_out):
    n_k = 240
    moved = jnp.concatenate([m0[...], m1[...], m2[...]], axis=1)
    res = nn_dot(moved, jnp.concatenate([sel_a[...], sel_b[...]], axis=1))
    for rr, g_in in enumerate((g_a, g_b)):
        for x in range(8):
            g_out[rr, :, x * 128 : (x + 1) * 128] = (
                g_in[:, x * 128 : (x + 1) * 128]
                + res[x * n_k : (x + 1) * n_k, rr * 128 : (rr + 1) * 128]
            )


def reach_kernel(*refs):
    blocks = refs[:4]
    coupling, own, other = refs[4:]
    me = lax.axis_index("grp")
    lanes = iota((32, 128), 1)
    outs = []
    for target in (me, me + 1 - 2 * lax.rem(me, 2)):
        row_at = pl.multiple_of(target * 32, 32)
        total = jnp.zeros((128, 128), F32)
        for k in range(4):
            gs = lax.rem(me + 8 - 2 * k, 8)
            col_at = pl.multiple_of(gs // 4 * 128, 128)
            window = coupling[pl.ds(row_at, 32), pl.ds(col_at, 128)]
            same = lanes + col_at == iota((32, 128), 0) + row_at
            window = jnp.where(same, 0.0, window)
            parts = []
            for q in range(4):
                by = lax.rem(q * 32 + 128 - lax.rem(gs, 4) * 32, 128)
                turned = pltpu.roll(window, by, 1)
                parts.append(jnp.where((lanes >= q * 32) & (lanes < q * 32 + 32), turned, 0.0))
            total = total + lax.dot_general(
                blocks[k][...],
                jnp.concatenate(parts, axis=0),
                (((1,), (1,)), ((), ())),
                preferred_element_type=F32,
                precision=lax.Precision.HIGHEST,
            )
        outs.append(total)
    own[...] = outs[0]
    other[...] = outs[1]


def final_kernel(*refs):
    gs = refs[:4]
    rts = refs[4:12]
    fars = refs[12:16]
    far_axial, cid, crot, incident, mie, out, gb, fin, fsum = refs[16:]
    n_k = 240
    z = lax.axis_index("mem") // 4
    for k in range(4):
        at = pl.multiple_of(lax.rem(z + 4 - k, 4) * 128, 128)
        fin[pl.ds(at, 128), :] = fars[k][...]
    mat = far_axial[...].reshape(2 * n_k, n_k)
    ids = jnp.broadcast_to(cid[...], (n_k, 128))
    for xh in range(2):
        cluster = packed_complex(mat, fin[xh * n_k : (xh + 1) * n_k, :])
        for q in range(4):
            fsum[2 * q + xh] = jnp.take_along_axis(cluster, ids + q * 32, axis=1)
    turn = jnp.broadcast_to(crot[...], (n_k, 128))
    pad = jnp.zeros((16, 1024), BF)
    for r in range(8):
        mine = turn == r
        for x in range(8):
            total = gs[r // 2][r % 2, :, x * 128 : (x + 1) * 128] + jnp.where(mine, fsum[x], 0.0)
            gb[r * 256 : r * 256 + n_k, x * 128 : (x + 1) * 128] = total.astype(BF)
        gb[r * 256 + n_k : (r + 1) * 256, :] = pad
    field = nn_dot(jnp.concatenate([t[...] for t in rts], axis=1), gb[...])
    mie_re = jnp.transpose(jnp.broadcast_to(mie[0:1, :], (128, n_k)))
    mie_im = jnp.transpose(jnp.broadcast_to(mie[1:2, :], (128, n_k)))
    for d in range(4):
        re = incident[d] + field[:, d * 128 : (d + 1) * 128]
        im = incident[4 + d] + field[:, (4 + d) * 128 : (5 + d) * 128]
        out[d] = mie_re * re - mie_im * im
        out[4 + d] = mie_re * im + mie_im * re


def params(mib):
    return pltpu.CompilerParams(vmem_limit_bytes=mib << 20)


def cost(flops, bytes_accessed):
    return pl.CostEstimate(flops=int(flops), transcendentals=0, bytes_accessed=int(bytes_accessed))


def on_device(
    coefficients,
    incident,
    mie_coeffs,
    rot_table,
    axial_shells,
    up_axial,
    far_axial,
    coupling,
    cluster_ids,
    center_rot,
    pair_col,
    pair_rot,
    send_col,
):
    sds = jax.ShapeDtypeStruct
    cid = cluster_ids.reshape(1, 128)
    crot = center_rot.reshape(1, 128)
    first = pl.pallas_call(
        send_kernel,
        out_shape=[sds((1920, 128), BF)] * 8 + [sds((960, 128), BF)] * 6 + [sds((128, 128), F32)] * 4,
        in_specs=[pl.BlockSpec(memory_space=pltpu.MemorySpace.HBM)] * 6,
        out_specs=[VM] * 18,
        scratch_shapes=[
            pltpu.VMEM((8, 240, 128), F32),
            pltpu.VMEM((8, 240, 240), BF),
            pltpu.VMEM((6, 64), I32),
            pltpu.VMEM((1, 128), I32),
            pltpu.VMEM((1, 128), I32),
            pltpu.VMEM((2, 240, 240), BF),
            pltpu.VMEM((240, 1024), BF),
            pltpu.VMEM((1024, 512), BF),
            pltpu.VMEM((512, 128), F32),
            pltpu.SemaphoreType.DMA((6,)),
        ],
        compiler_params=params(24),
        name="send",
    )(*[pltpu.with_memory_space_constraint(v, pltpu.HBM) for v in (coefficients, rot_table, send_col, crot, cid, up_axial)])
    pools = first[:8]
    sends = first[8:14]
    fars = first[14:18]
    moves = (("mem", 1), ("mem", -1), ("mem", 2), ("mem", -2), ("grp", 1), ("grp", -1))
    got = []
    for p in range(6):
        got.append(shifted(sends[p], *moves[p]))
    acc = fars[0]
    for k in (2, 1, 3):
        come = shifted(fars[k], "mem", 4 * k)
        acc = acc + come
    blocks = [acc]
    for k in (1, 2, 3):
        blocks.append(shifted(acc, "grp", 2 * k))
    mine, theirs = pl.pallas_call(
        reach_kernel,
        out_shape=[sds((128, 128), F32)] * 2,
        in_specs=[VM] * 5,
        out_specs=[VM] * 2,
        compiler_params=params(2),
        name="reach",
    )(*blocks, coupling)
    come = moved_by(theirs, "grp", lambda i: i ^ 1)
    part = mine + come
    total = part
    for k in (2, 1, 3):
        total = total + moved_by(part, "mem", lambda i: i // 4 * 4 + (i + k) % 4)
    reached = [total.astype(BF)]
    for k in (1, 2, 3):
        reached.append(shifted(reached[0], "mem", 4 * k))
    g_own, sels, rts = [], [], []
    mats = None
    for r in range(8):
        res = pl.pallas_call(
            lambda *refs, r=r: own_kernel(r, *refs),
            out_shape=[sds((240, 1024), F32), sds((1152, 128), BF), sds((240, 256), BF)]
            + ([sds((480, 768), BF)] if r == 0 else []),
            in_specs=[VM] * 5,
            out_specs=[VM] * (4 if r == 0 else 3),
            scratch_shapes=[pltpu.VMEM((768, 1024), BF)],
            compiler_params=params(20),
            cost_estimate=cost(1.26e9, 3e6),
        )(pools[r], pair_col, pair_rot, rot_table, axial_shells if r == 0 else mats)
        if r == 0:
            mats = res[3]
        g_own.append(res[0])
        sels.append(res[1])
        rts.append(res[2])
    lifted = []
    for j in range(3):
        lifted.append(
            pl.pallas_call(
                lift_kernel,
                out_shape=sds((1920, 384), BF),
                in_specs=[VM] * 3,
                out_specs=VM,
                scratch_shapes=[pltpu.VMEM((240, 1024), BF)],
                compiler_params=params(20),
                cost_estimate=cost(0.7e9, 3e6),
            )(got[2 * j], got[2 * j + 1], axial_shells)
        )
    totals = []
    for q in range(4):
        totals.append(
            pl.pallas_call(
                recv_kernel,
                out_shape=sds((2, 240, 1024), F32),
                in_specs=[VM] * 7,
                out_specs=VM,
                compiler_params=params(20),
                cost_estimate=cost(1.2e9, 8e6),
            )(*lifted, sels[2 * q], sels[2 * q + 1], g_own[2 * q], g_own[2 * q + 1])
        )
    return pl.pallas_call(
        final_kernel,
        out_shape=sds((8, 240, 128), F32),
        in_specs=[VM] * 21,
        out_specs=VM,
        scratch_shapes=[
            pltpu.VMEM((2048, 1024), BF),
            pltpu.VMEM((512, 128), BF),
            pltpu.VMEM((8, 240, 128), F32),
        ],
        compiler_params=params(20),
        name="final",
    )(*totals, *rts, *reached, far_axial, cid, crot, incident, mie_coeffs)


def solution(mesh):
    in_specs = (
        P(None, None, ("grp", "mem")),
        P(None, None, ("grp", "mem")),
        P(),
        P(),
        P(),
        P(),
        P(),
        P(),
        P(("grp", "mem")),
        P(("grp", "mem")),
        P(None, ("grp", "mem")),
        P(None, ("grp", "mem")),
        P(("grp", "mem"), None),
    )
    out_specs = P(None, None, ("grp", "mem"))

    return jax.shard_map(
        on_device, mesh=mesh, in_specs=in_specs, out_specs=out_specs, check_vma=False
    )
```

```python
import jax
import jax.numpy as jnp
from jax import lax
from jax.experimental import pallas as pl
from jax.experimental.pallas import tpu as pltpu
from jax.sharding import PartitionSpec as P


BF = jnp.bfloat16
F32 = jnp.float32
I32 = jnp.int32
VM = pl.BlockSpec(memory_space=pltpu.VMEM)


def nn_dot(a, b):
    return lax.dot_general(a, b, (((1,), (0,)), ((), ())), preferred_element_type=F32)


def iota(shape, dim):
    return lax.broadcasted_iota(I32, shape, dim)


def moved_by(value, axis, target):
    length = lax.axis_size(axis)
    return lax.ppermute(value, axis, [(i, target(i)) for i in range(length)])


def flipped(value, axis, bits):
    return moved_by(value, axis, lambda i: i ^ bits)


def upper_sides():
    m = lax.axis_index("mem")
    g = lax.axis_index("grp")
    return lax.rem(m, 2), lax.rem(m // 2, 2), lax.rem(g, 2)


def packed_complex(mat, cols):
    k = mat.shape[0] // 2
    both = nn_dot(mat, cols)
    sign = jnp.where(iota((k, 128), 1) < 64, -1.0, 1.0).astype(F32)
    return both[:k] + pltpu.roll(both[k:], 64, 1) * sign


def send_kernel(coef_h, rot_h, send_h, crot_h, cid_h, up_h, *rest):
    pools = rest[:8]
    outs = rest[8:14]
    fars = rest[14:16]
    coef, rot, send, crot, cid, up, xs, sel, whole, sems = rest[16:]
    pairs = ((coef_h, coef), (rot_h, rot), (send_h, send), (crot_h, crot), (cid_h, cid), (up_h, up))
    copies = [pltpu.make_async_copy(src, dst, sems.at[i]) for i, (src, dst) in enumerate(pairs)]
    for copy in copies:
        copy.start()
    n_x, n_k, n_i = coef.shape
    n_r = rot.shape[0]
    for i in (2, 3, 4):
        copies[i].wait()
    rows = iota((n_r * n_i, 128), 0)
    for q, upper in enumerate(upper_sides()):
        up_row, down_row = send[2 * q : 2 * q + 1, :], send[2 * q + 1 : 2 * q + 2, :]
        ids = jnp.where(
            upper == 1,
            jnp.concatenate([down_row, up_row], axis=1),
            jnp.concatenate([up_row, down_row], axis=1),
        )
        sel[:, q * 128 : (q + 1) * 128] = jnp.where(rows == ids, 1.0, 0.0).astype(BF)
    key = (crot[...] * 32 + cid[...]).astype(F32)
    key_t = jnp.transpose(jnp.broadcast_to(key, (n_i, n_i)))
    lanes = iota((n_i, n_i), 1)
    for r in range(n_r):
        hit = (key_t == (lanes + r * 32).astype(F32)) & (lanes < 32)
        sel[r * n_i : (r + 1) * n_i, 384:512] = jnp.where(hit, 1.0, 0.0).astype(BF)
    for i in (0, 1, 5):
        copies[i].wait()
    for x in range(n_x):
        xs[:, x * n_i : (x + 1) * n_i] = coef[x].astype(BF)
    x_all = xs[...]
    for r in range(n_r):
        turned = nn_dot(rot[r], x_all).astype(BF)
        for x in range(n_x):
            pools[r][x * n_k : (x + 1) * n_k, :] = turned[:, x * n_i : (x + 1) * n_i]
    half = n_x // 2 * n_k
    real = nn_dot(jnp.concatenate([p[:half, :] for p in pools], axis=1), sel[...])
    imag = nn_dot(jnp.concatenate([p[half:, :] for p in pools], axis=1), sel[...])
    low = iota((half, 128), 1) < 64
    for q in range(3):
        re = real[:, q * 128 : (q + 1) * 128]
        im = imag[:, q * 128 : (q + 1) * 128]
        outs[2 * q][...] = jnp.where(low, re, pltpu.roll(im, 64, 1)).astype(BF)
        outs[2 * q + 1][...] = jnp.where(low, pltpu.roll(re, 64, 1), im).astype(BF)
    mat = up[...].reshape(2 * n_k, n_k)
    for xh in range(2):
        total = None
        for q in range(4):
            x = 2 * q + xh
            src = real if x < 4 else imag
            part = src[(x % 4) * n_k : (x % 4 + 1) * n_k, 384:512]
            part = pltpu.roll(part, 32 * q, 1) if q else part
            total = part if total is None else total + part
        hi = total.astype(BF)
        rem = total - hi.astype(F32)
        mid = rem.astype(BF)
        lo = (rem - mid.astype(F32)).astype(BF)
        whole[xh * n_k : (xh + 1) * n_k, :] = (
            packed_complex(mat, lo) + packed_complex(mat, mid) + packed_complex(mat, hi)
        )
    whole[2 * n_k :, :] = jnp.zeros((512 - 2 * n_k, 128), F32)
    place = lax.rem(lax.axis_index("mem"), 4)
    for k, flip in enumerate((0, 1, 3, 2)):
        at = pl.multiple_of(lax.bitwise_xor(place, flip) * 128, 128)
        fars[k // 2][k % 2 * 128 : k % 2 * 128 + 128, :] = whole[pl.ds(at, 128), :]


def own_kernel(r, *refs):
    if r == 0:
        pool, pcol, prot, rot, axial, g_out, sel_out, rt_out, mats, stack = refs
    else:
        pool, pcol, prot, rot, mats, g_out, sel_out, rt_out, stack = refs
    n_k = 240
    n_i = pcol.shape[1]
    if r == 0:
        mats[...] = jnp.zeros_like(mats)
        for s in range(3):
            mats[:, s * 256 : s * 256 + n_k] = axial[s].reshape(2 * n_k, n_k)
    for s in range(3):
        stack[s * 256 + n_k : (s + 1) * 256, :] = jnp.zeros((16, 8 * n_i), BF)
    rt_out[...] = jnp.zeros_like(rt_out)
    rt_out[:, :n_k] = jnp.transpose(rot[r].astype(F32)).astype(BF)
    js = iota((n_i, n_i), 0)
    counts = []
    for s in range(3):
        total = jnp.zeros((n_i, n_i), F32)
        for t in range(8):
            row = pcol[s * 8 + t : s * 8 + t + 1, :]
            total = total + jnp.where(row == js + r * n_i, 1.0, 0.0)
        counts.append(total.astype(BF))
    taken = nn_dot(pool[...], jnp.concatenate(counts, axis=1)).astype(BF)
    for s in range(3):
        for x in range(8):
            stack[s * 256 : s * 256 + n_k, x * n_i : (x + 1) * n_i] = taken[
                x * n_k : (x + 1) * n_k, s * n_i : (s + 1) * n_i
            ]
    both = nn_dot(mats[...], stack[...])
    half = 4 * n_i
    g_out[:, :half] = both[:n_k, :half] - both[n_k:, half:]
    g_out[:, half:] = both[n_k:, :half] + both[:n_k, half:]
    keys = jnp.where(pcol[...] >= 1024, pcol[...] - 1024 + prot[...] * 384, -1)
    for pair, upper in enumerate(upper_sides()):
        cols = lax.bitwise_xor(js, 64 - 64 * upper) + pair * 128 + r * 384
        for s in range(3):
            total = jnp.zeros((n_i, n_i), F32)
            for t in range(8):
                row = keys[s * 8 + t : s * 8 + t + 1, :]
                total = total + jnp.where(row == cols, 1.0, 0.0)
            at = (pair * 3 + s) * 128
            sel_out[at : at + 128, :] = total.astype(BF)


def lift_kernel(first, second, axial, moved, xs):
    n_k = 240
    low = iota((n_k, 128), 1) < 64
    for d in range(4):
        a = first[d * n_k : (d + 1) * n_k, :].astype(F32)
        b = second[d * n_k : (d + 1) * n_k, :].astype(F32)
        at = d * 128
        xs[:, at : at + 128] = jnp.where(low, a, pltpu.roll(b, 64, 1)).astype(BF)
        xs[:, 512 + at : 512 + at + 128] = jnp.where(low, pltpu.roll(a, 64, 1), b).astype(BF)
    for s in range(3):
        both = nn_dot(axial[s].reshape(2 * n_k, n_k), xs[...])
        real = (both[:n_k, :512] - both[n_k:, 512:]).astype(BF)
        imag = (both[n_k:, :512] + both[:n_k, 512:]).astype(BF)
        lane = s * 128
        for d in range(4):
            at = d * 128
            moved[d * n_k : (d + 1) * n_k, lane : lane + 128] = real[:, at : at + 128]
            moved[(4 + d) * n_k : (5 + d) * n_k, lane : lane + 128] = imag[:, at : at + 128]


def recv_kernel(m0, m1, m2, sel_a, sel_b, g_a, g_b, g_out):
    n_k = 240
    moved = jnp.concatenate([m0[...], m1[...], m2[...]], axis=1)
    res = nn_dot(moved, jnp.concatenate([sel_a[...], sel_b[...]], axis=1))
    for rr, g_in in enumerate((g_a, g_b)):
        for x in range(8):
            g_out[rr, :, x * 128 : (x + 1) * 128] = (
                g_in[:, x * 128 : (x + 1) * 128]
                + res[x * n_k : (x + 1) * n_k, rr * 128 : (rr + 1) * 128]
            )


def reach_kernel(*refs):
    halves = refs[:2]
    coupling, own, other = refs[2:]
    me = lax.axis_index("grp")
    lanes = iota((32, 128), 1)
    outs = []
    for target in (me, lax.bitwise_xor(me, 1)):
        row_at = pl.multiple_of(target * 32, 32)
        total = jnp.zeros((128, 128), F32)
        for k, flip in enumerate((0, 2, 6, 4)):
            gs = lax.bitwise_xor(me, flip)
            col_at = pl.multiple_of(gs // 4 * 128, 128)
            window = coupling[pl.ds(row_at, 32), pl.ds(col_at, 128)]
            same = lanes + col_at == iota((32, 128), 0) + row_at
            window = jnp.where(same, 0.0, window)
            parts = []
            for q in range(4):
                by = lax.rem(q * 32 + 128 - lax.rem(gs, 4) * 32, 128)
                turned = pltpu.roll(window, by, 1)
                parts.append(jnp.where((lanes >= q * 32) & (lanes < q * 32 + 32), turned, 0.0))
            total = total + lax.dot_general(
                halves[k // 2][k % 2 * 128 : k % 2 * 128 + 128, :],
                jnp.concatenate(parts, axis=0),
                (((1,), (1,)), ((), ())),
                preferred_element_type=F32,
                precision=lax.Precision.HIGHEST,
            )
        outs.append(total)
    own[...] = outs[0]
    other[...] = outs[1]


def final_kernel(*refs):
    gs = refs[:4]
    rts = refs[4:12]
    fars = refs[12:14]
    far_axial, cid, crot, incident, mie, out, gb, fin, fsum = refs[14:]
    n_k = 240
    place = lax.rem(lax.axis_index("mem"), 4)
    for k, flip in enumerate((0, 1, 3, 2)):
        at = pl.multiple_of(lax.bitwise_xor(place, flip) * 128, 128)
        fin[pl.ds(at, 128), :] = fars[k // 2][k % 2 * 128 : k % 2 * 128 + 128, :]
    mat = far_axial[...].reshape(2 * n_k, n_k)
    ids = jnp.broadcast_to(cid[...], (n_k, 128))
    for xh in range(2):
        cluster = packed_complex(mat, fin[xh * n_k : (xh + 1) * n_k, :])
        for q in range(4):
            fsum[2 * q + xh] = jnp.take_along_axis(cluster, ids + q * 32, axis=1)
    turn = jnp.broadcast_to(crot[...], (n_k, 128))
    pad = jnp.zeros((16, 1024), BF)
    for r in range(8):
        mine = turn == r
        for x in range(8):
            total = gs[r // 2][r % 2, :, x * 128 : (x + 1) * 128] + jnp.where(mine, fsum[x], 0.0)
            gb[r * 256 : r * 256 + n_k, x * 128 : (x + 1) * 128] = total.astype(BF)
        gb[r * 256 + n_k : (r + 1) * 256, :] = pad
    field = nn_dot(jnp.concatenate([t[...] for t in rts], axis=1), gb[...])
    mie_re = jnp.transpose(jnp.broadcast_to(mie[0:1, :], (128, n_k)))
    mie_im = jnp.transpose(jnp.broadcast_to(mie[1:2, :], (128, n_k)))
    for d in range(4):
        re = incident[d] + field[:, d * 128 : (d + 1) * 128]
        im = incident[4 + d] + field[:, (4 + d) * 128 : (5 + d) * 128]
        out[d] = mie_re * re - mie_im * im
        out[4 + d] = mie_re * im + mie_im * re


def params(mib):
    return pltpu.CompilerParams(vmem_limit_bytes=mib << 20)


def cost(flops, bytes_accessed):
    return pl.CostEstimate(flops=int(flops), transcendentals=0, bytes_accessed=int(bytes_accessed))


def on_device(
    coefficients,
    incident,
    mie_coeffs,
    rot_table,
    axial_shells,
    up_axial,
    far_axial,
    coupling,
    cluster_ids,
    center_rot,
    pair_col,
    pair_rot,
    send_col,
):
    sds = jax.ShapeDtypeStruct
    cid = cluster_ids.reshape(1, 128)
    crot = center_rot.reshape(1, 128)
    first = pl.pallas_call(
        send_kernel,
        out_shape=[sds((1920, 128), BF)] * 8 + [sds((960, 128), BF)] * 6 + [sds((256, 128), F32)] * 2,
        in_specs=[pl.BlockSpec(memory_space=pltpu.MemorySpace.HBM)] * 6,
        out_specs=[VM] * 16,
        scratch_shapes=[
            pltpu.VMEM((8, 240, 128), F32),
            pltpu.VMEM((8, 240, 240), BF),
            pltpu.VMEM((6, 64), I32),
            pltpu.VMEM((1, 128), I32),
            pltpu.VMEM((1, 128), I32),
            pltpu.VMEM((2, 240, 240), BF),
            pltpu.VMEM((240, 1024), BF),
            pltpu.VMEM((1024, 512), BF),
            pltpu.VMEM((512, 128), F32),
            pltpu.SemaphoreType.DMA((6,)),
        ],
        compiler_params=params(24),
        name="send",
    )(*[pltpu.with_memory_space_constraint(v, pltpu.HBM) for v in (coefficients, rot_table, send_col, crot, cid, up_axial)])
    pools = first[:8]
    sends = first[8:14]
    near_blocks, far_blocks = first[14:]
    got = []
    for q, (axis, bit) in enumerate((("mem", 1), ("mem", 2), ("grp", 1))):
        got.append(flipped(sends[2 * q], axis, bit))
        size = lax.axis_size(axis)
        got.append(
            moved_by(sends[2 * q + 1], axis, lambda i: (i + (bit if i & bit else -bit)) % size)
        )
    come = flipped(far_blocks, "mem", 3)
    come_next = flipped(near_blocks[128:] + come[128:], "mem", 1)
    acc = near_blocks[:128] + come[:128] + come_next
    come = flipped(acc, "grp", 2)
    pair = jnp.concatenate([acc, come], axis=0)
    come = flipped(pair, "grp", 6)
    mine, theirs = pl.pallas_call(
        reach_kernel,
        out_shape=[sds((128, 128), F32)] * 2,
        in_specs=[VM] * 3,
        out_specs=[VM] * 2,
        compiler_params=params(2),
        name="reach",
    )(pair, come, coupling)
    come = flipped(theirs, "grp", 1)
    total = mine + come
    for flip in (4, 12):
        come = flipped(total, "mem", flip)
        total = total + come
    total = total.astype(BF)
    come = flipped(total, "mem", 1)
    reached = [jnp.concatenate([total, come], axis=0)]
    reached.append(flipped(reached[0], "mem", 3))
    g_own, sels, rts = [], [], []
    mats = None
    for r in range(8):
        res = pl.pallas_call(
            lambda *refs, r=r: own_kernel(r, *refs),
            out_shape=[sds((240, 1024), F32), sds((1152, 128), BF), sds((240, 256), BF)]
            + ([sds((480, 768), BF)] if r == 0 else []),
            in_specs=[VM] * 5,
            out_specs=[VM] * (4 if r == 0 else 3),
            scratch_shapes=[pltpu.VMEM((768, 1024), BF)],
            compiler_params=params(20),
            cost_estimate=cost(1.26e9, 3e6),
        )(pools[r], pair_col, pair_rot, rot_table, axial_shells if r == 0 else mats)
        if r == 0:
            mats = res[3]
        g_own.append(res[0])
        sels.append(res[1])
        rts.append(res[2])
    lifted = []
    for j in range(3):
        lifted.append(
            pl.pallas_call(
                lift_kernel,
                out_shape=sds((1920, 384), BF),
                in_specs=[VM] * 3,
                out_specs=VM,
                scratch_shapes=[pltpu.VMEM((240, 1024), BF)],
                compiler_params=params(20),
                cost_estimate=cost(0.7e9, 3e6),
            )(got[2 * j], got[2 * j + 1], axial_shells)
        )
    totals = []
    for q in range(4):
        totals.append(
            pl.pallas_call(
                recv_kernel,
                out_shape=sds((2, 240, 1024), F32),
                in_specs=[VM] * 7,
                out_specs=VM,
                compiler_params=params(20),
                cost_estimate=cost(1.2e9, 8e6),
            )(*lifted, sels[2 * q], sels[2 * q + 1], g_own[2 * q], g_own[2 * q + 1])
        )
    return pl.pallas_call(
        final_kernel,
        out_shape=sds((8, 240, 128), F32),
        in_specs=[VM] * 19,
        out_specs=VM,
        scratch_shapes=[
            pltpu.VMEM((2048, 1024), BF),
            pltpu.VMEM((512, 128), BF),
            pltpu.VMEM((8, 240, 128), F32),
        ],
        compiler_params=params(20),
        name="final",
    )(*totals, *rts, *reached, far_axial, cid, crot, incident, mie_coeffs)


def solution(mesh):
    in_specs = (
        P(None, None, ("grp", "mem")),
        P(None, None, ("grp", "mem")),
        P(),
        P(),
        P(),
        P(),
        P(),
        P(),
        P(("grp", "mem")),
        P(("grp", "mem")),
        P(None, ("grp", "mem")),
        P(None, ("grp", "mem")),
        P(("grp", "mem"), None),
    )
    out_specs = P(None, None, ("grp", "mem"))

    return jax.shard_map(
        on_device, mesh=mesh, in_specs=in_specs, out_specs=out_specs, check_vma=False
    )
```

```python
import jax
import jax.numpy as jnp
from jax import lax
from jax.experimental import pallas as pl
from jax.experimental.pallas import tpu as pltpu
from jax.sharding import PartitionSpec as P


BF = jnp.bfloat16
F32 = jnp.float32
I32 = jnp.int32
VM = pl.BlockSpec(memory_space=pltpu.VMEM)


def nn_dot(a, b):
    return lax.dot_general(a, b, (((1,), (0,)), ((), ())), preferred_element_type=F32)


def iota(shape, dim):
    return lax.broadcasted_iota(I32, shape, dim)


def moved_by(value, axis, target):
    length = lax.axis_size(axis)
    return lax.ppermute(value, axis, [(i, target(i)) for i in range(length)])


def flipped(value, axis, bits):
    return moved_by(value, axis, lambda i: i ^ bits)


def upper_sides():
    m = lax.axis_index("mem")
    g = lax.axis_index("grp")
    return lax.rem(m, 2), lax.rem(m // 2, 2), lax.rem(g, 2)


def packed_complex(mat, cols):
    k = mat.shape[0] // 2
    both = nn_dot(mat, cols)
    sign = jnp.where(iota((k, 128), 1) < 64, -1.0, 1.0).astype(F32)
    return both[:k] + pltpu.roll(both[k:], 64, 1) * sign


def send_kernel(coef_h, rot_h, send_h, crot_h, cid_h, up_h, *rest):
    pools = rest[:8]
    outs = rest[8:14]
    fars = rest[14:16]
    coef, rot, send, crot, cid, up, xs, sel, whole, sems = rest[16:]
    pairs = ((coef_h, coef), (rot_h, rot), (send_h, send), (crot_h, crot), (cid_h, cid), (up_h, up))
    copies = [pltpu.make_async_copy(src, dst, sems.at[i]) for i, (src, dst) in enumerate(pairs)]
    for i in (2, 3, 4, 0, 1, 5):
        copies[i].start()
    n_x, n_k, n_i = coef.shape
    n_r = rot.shape[0]
    for i in (2, 3, 4):
        copies[i].wait()
    rows = iota((n_r * n_i, 128), 0)
    for q, upper in enumerate(upper_sides()):
        up_row, down_row = send[2 * q : 2 * q + 1, :], send[2 * q + 1 : 2 * q + 2, :]
        ids = jnp.where(
            upper == 1,
            jnp.concatenate([down_row, up_row], axis=1),
            jnp.concatenate([up_row, down_row], axis=1),
        )
        sel[:, q * 128 : (q + 1) * 128] = jnp.where(rows == ids, 1.0, 0.0).astype(BF)
    key = (crot[...] * 32 + cid[...]).astype(F32)
    key_t = jnp.transpose(jnp.broadcast_to(key, (n_i, n_i)))
    lanes = iota((n_i, n_i), 1)
    for r in range(n_r):
        hit = (key_t == (lanes + r * 32).astype(F32)) & (lanes < 32)
        sel[r * n_i : (r + 1) * n_i, 384:512] = jnp.where(hit, 1.0, 0.0).astype(BF)
    for i in (0, 1, 5):
        copies[i].wait()
    for x in range(n_x):
        xs[:, x * n_i : (x + 1) * n_i] = coef[x].astype(BF)
    x_all = xs[...]
    for r in range(n_r):
        turned = nn_dot(rot[r], x_all).astype(BF)
        for x in range(n_x):
            pools[r][x * n_k : (x + 1) * n_k, :] = turned[:, x * n_i : (x + 1) * n_i]
    half = n_x // 2 * n_k
    real = nn_dot(jnp.concatenate([p[:half, :] for p in pools], axis=1), sel[...])
    imag = nn_dot(jnp.concatenate([p[half:, :] for p in pools], axis=1), sel[...])
    low = iota((half, 128), 1) < 64
    for q in range(3):
        re = real[:, q * 128 : (q + 1) * 128]
        im = imag[:, q * 128 : (q + 1) * 128]
        outs[2 * q][...] = jnp.where(low, re, pltpu.roll(im, 64, 1)).astype(BF)
        outs[2 * q + 1][...] = jnp.where(low, pltpu.roll(re, 64, 1), im).astype(BF)
    mat = up[...].reshape(2 * n_k, n_k)
    for xh in range(2):
        total = None
        for q in range(4):
            x = 2 * q + xh
            src = real if x < 4 else imag
            part = src[(x % 4) * n_k : (x % 4 + 1) * n_k, 384:512]
            part = pltpu.roll(part, 32 * q, 1) if q else part
            total = part if total is None else total + part
        hi = total.astype(BF)
        rem = total - hi.astype(F32)
        mid = rem.astype(BF)
        lo = (rem - mid.astype(F32)).astype(BF)
        whole[xh * n_k : (xh + 1) * n_k, :] = (
            packed_complex(mat, lo) + packed_complex(mat, mid) + packed_complex(mat, hi)
        )
    whole[2 * n_k :, :] = jnp.zeros((512 - 2 * n_k, 128), F32)
    place = lax.rem(lax.axis_index("mem"), 4)
    for k, flip in enumerate((0, 1, 3, 2)):
        at = pl.multiple_of(lax.bitwise_xor(place, flip) * 128, 128)
        fars[k // 2][k % 2 * 128 : k % 2 * 128 + 128, :] = whole[pl.ds(at, 128), :]


def own_kernel(r, *refs):
    if r == 0:
        pool, pcol, prot, rot, axial, g_out, sel_out, rt_out, mats, stack = refs
    else:
        pool, pcol, prot, rot, mats, g_out, sel_out, rt_out, stack = refs
    n_k = 240
    n_i = pcol.shape[1]
    if r == 0:
        mats[...] = jnp.zeros_like(mats)
        for s in range(3):
            mats[:, s * 256 : s * 256 + n_k] = axial[s].reshape(2 * n_k, n_k)
    for s in range(3):
        stack[s * 256 + n_k : (s + 1) * 256, :] = jnp.zeros((16, 8 * n_i), BF)
    rt_out[...] = jnp.zeros_like(rt_out)
    rt_out[:, :n_k] = jnp.transpose(rot[r].astype(F32)).astype(BF)
    js = iota((n_i, n_i), 0)
    counts = []
    for s in range(3):
        total = jnp.zeros((n_i, n_i), F32)
        for t in range(8):
            row = pcol[s * 8 + t : s * 8 + t + 1, :]
            total = total + jnp.where(row == js + r * n_i, 1.0, 0.0)
        counts.append(total.astype(BF))
    taken = nn_dot(pool[...], jnp.concatenate(counts, axis=1)).astype(BF)
    for s in range(3):
        for x in range(8):
            stack[s * 256 : s * 256 + n_k, x * n_i : (x + 1) * n_i] = taken[
                x * n_k : (x + 1) * n_k, s * n_i : (s + 1) * n_i
            ]
    both = nn_dot(mats[...], stack[...])
    half = 4 * n_i
    g_out[:, :half] = both[:n_k, :half] - both[n_k:, half:]
    g_out[:, half:] = both[n_k:, :half] + both[:n_k, half:]
    keys = jnp.where(pcol[...] >= 1024, pcol[...] - 1024 + prot[...] * 384, -1)
    for pair, upper in enumerate(upper_sides()):
        cols = lax.bitwise_xor(js, 64 - 64 * upper) + pair * 128 + r * 384
        for s in range(3):
            total = jnp.zeros((n_i, n_i), F32)
            for t in range(8):
                row = keys[s * 8 + t : s * 8 + t + 1, :]
                total = total + jnp.where(row == cols, 1.0, 0.0)
            at = (pair * 3 + s) * 128
            sel_out[at : at + 128, :] = total.astype(BF)


def lift_kernel(first, second, axial, moved, xs):
    n_k = 240
    low = iota((n_k, 128), 1) < 64
    for d in range(4):
        a = first[d * n_k : (d + 1) * n_k, :].astype(F32)
        b = second[d * n_k : (d + 1) * n_k, :].astype(F32)
        at = d * 128
        xs[:, at : at + 128] = jnp.where(low, a, pltpu.roll(b, 64, 1)).astype(BF)
        xs[:, 512 + at : 512 + at + 128] = jnp.where(low, pltpu.roll(a, 64, 1), b).astype(BF)
    for s in range(3):
        both = nn_dot(axial[s].reshape(2 * n_k, n_k), xs[...])
        real = (both[:n_k, :512] - both[n_k:, 512:]).astype(BF)
        imag = (both[n_k:, :512] + both[:n_k, 512:]).astype(BF)
        lane = s * 128
        for d in range(4):
            at = d * 128
            moved[d * n_k : (d + 1) * n_k, lane : lane + 128] = real[:, at : at + 128]
            moved[(4 + d) * n_k : (5 + d) * n_k, lane : lane + 128] = imag[:, at : at + 128]


def recv_kernel(m0, m1, m2, sel_a, sel_b, g_a, g_b, g_out):
    n_k = 240
    moved = jnp.concatenate([m0[...], m1[...], m2[...]], axis=1)
    res = nn_dot(moved, jnp.concatenate([sel_a[...], sel_b[...]], axis=1))
    for rr, g_in in enumerate((g_a, g_b)):
        for x in range(8):
            g_out[rr, :, x * 128 : (x + 1) * 128] = (
                g_in[:, x * 128 : (x + 1) * 128]
                + res[x * n_k : (x + 1) * n_k, rr * 128 : (rr + 1) * 128]
            )


def reach_kernel(*refs):
    halves = refs[:2]
    coupling, own, other = refs[2:]
    me = lax.axis_index("grp")
    lanes = iota((32, 128), 1)
    rows = []
    for target in (me, lax.bitwise_xor(me, 1)):
        row_at = pl.multiple_of(target * 32, 32)
        lines = [[] for _ in range(4)]
        for flip in (0, 2, 6, 4):
            gs = lax.bitwise_xor(me, flip)
            col_at = pl.multiple_of(gs // 4 * 128, 128)
            window = coupling[pl.ds(row_at, 32), pl.ds(col_at, 128)]
            same = lanes + col_at == iota((32, 128), 0) + row_at
            window = jnp.where(same, 0.0, window)
            for q in range(4):
                by = lax.rem(q * 32 + 128 - lax.rem(gs, 4) * 32, 128)
                turned = pltpu.roll(window, by, 1)
                lines[q].append(jnp.where((lanes >= q * 32) & (lanes < q * 32 + 32), turned, 0.0))
        rows += [jnp.concatenate(line, axis=1) for line in lines]
    blocks = [half[at : at + 128, :] for half in halves for at in (0, 128)]
    both = lax.dot_general(
        jnp.concatenate(blocks, axis=1),
        jnp.concatenate(rows, axis=0),
        (((1,), (1,)), ((), ())),
        preferred_element_type=F32,
        precision=lax.Precision.HIGHEST,
    )
    own[...] = both[:, :128]
    other[...] = both[:, 128:]


def final_kernel(*refs):
    gs = refs[:4]
    rts = refs[4:12]
    fars = refs[12:14]
    far_axial, cid, crot, incident, mie, out, gb, fin, fsum = refs[14:]
    n_k = 240
    place = lax.rem(lax.axis_index("mem"), 4)
    for k, flip in enumerate((0, 1, 3, 2)):
        at = pl.multiple_of(lax.bitwise_xor(place, flip) * 128, 128)
        fin[pl.ds(at, 128), :] = fars[k // 2][k % 2 * 128 : k % 2 * 128 + 128, :]
    mat = far_axial[...].reshape(2 * n_k, n_k)
    ids = jnp.broadcast_to(cid[...], (n_k, 128))
    for xh in range(2):
        cluster = packed_complex(mat, fin[xh * n_k : (xh + 1) * n_k, :])
        for q in range(4):
            fsum[2 * q + xh] = jnp.take_along_axis(cluster, ids + q * 32, axis=1)
    turn = jnp.broadcast_to(crot[...], (n_k, 128))
    pad = jnp.zeros((16, 1024), BF)
    for r in range(8):
        mine = turn == r
        for x in range(8):
            total = gs[r // 2][r % 2, :, x * 128 : (x + 1) * 128] + jnp.where(mine, fsum[x], 0.0)
            gb[r * 256 : r * 256 + n_k, x * 128 : (x + 1) * 128] = total.astype(BF)
        gb[r * 256 + n_k : (r + 1) * 256, :] = pad
    field = nn_dot(jnp.concatenate([t[...] for t in rts], axis=1), gb[...])
    mie_re = jnp.transpose(jnp.broadcast_to(mie[0:1, :], (128, n_k)))
    mie_im = jnp.transpose(jnp.broadcast_to(mie[1:2, :], (128, n_k)))
    for d in range(4):
        re = incident[d] + field[:, d * 128 : (d + 1) * 128]
        im = incident[4 + d] + field[:, (4 + d) * 128 : (5 + d) * 128]
        out[d] = mie_re * re - mie_im * im
        out[4 + d] = mie_re * im + mie_im * re


def params(mib):
    return pltpu.CompilerParams(vmem_limit_bytes=mib << 20)


def cost(flops, bytes_accessed):
    return pl.CostEstimate(flops=int(flops), transcendentals=0, bytes_accessed=int(bytes_accessed))


def on_device(
    coefficients,
    incident,
    mie_coeffs,
    rot_table,
    axial_shells,
    up_axial,
    far_axial,
    coupling,
    cluster_ids,
    center_rot,
    pair_col,
    pair_rot,
    send_col,
):
    sds = jax.ShapeDtypeStruct
    cid = cluster_ids.reshape(1, 128)
    crot = center_rot.reshape(1, 128)
    first = pl.pallas_call(
        send_kernel,
        out_shape=[sds((1920, 128), BF)] * 8 + [sds((960, 128), BF)] * 6 + [sds((256, 128), F32)] * 2,
        in_specs=[pl.BlockSpec(memory_space=pltpu.MemorySpace.HBM)] * 6,
        out_specs=[VM] * 16,
        scratch_shapes=[
            pltpu.VMEM((8, 240, 128), F32),
            pltpu.VMEM((8, 240, 240), BF),
            pltpu.VMEM((6, 64), I32),
            pltpu.VMEM((1, 128), I32),
            pltpu.VMEM((1, 128), I32),
            pltpu.VMEM((2, 240, 240), BF),
            pltpu.VMEM((240, 1024), BF),
            pltpu.VMEM((1024, 512), BF),
            pltpu.VMEM((512, 128), F32),
            pltpu.SemaphoreType.DMA((6,)),
        ],
        compiler_params=params(24),
        name="send",
    )(*[pltpu.with_memory_space_constraint(v, pltpu.HBM) for v in (coefficients, rot_table, send_col, crot, cid, up_axial)])
    pools = first[:8]
    sends = first[8:14]
    near_blocks, far_blocks = first[14:]
    got = []
    for q, (axis, bit) in enumerate((("mem", 1), ("mem", 2), ("grp", 1))):
        got.append(flipped(sends[2 * q], axis, bit))
        size = lax.axis_size(axis)
        got.append(
            moved_by(sends[2 * q + 1], axis, lambda i: (i + (bit if i & bit else -bit)) % size)
        )
    come = flipped(far_blocks, "mem", 3)
    come_next = flipped(near_blocks[128:] + come[128:], "mem", 1)
    acc = near_blocks[:128] + come[:128] + come_next
    come = flipped(acc, "grp", 2)
    pair = jnp.concatenate([acc, come], axis=0)
    come = flipped(pair, "grp", 6)
    mine, theirs = pl.pallas_call(
        reach_kernel,
        out_shape=[sds((128, 128), F32)] * 2,
        in_specs=[VM] * 3,
        out_specs=[VM] * 2,
        compiler_params=params(2),
        name="reach",
    )(pair, come, coupling)
    come = flipped(theirs, "grp", 1)
    total = mine + come
    for flip in (4, 12):
        come = flipped(total, "mem", flip)
        total = total + come
    total = total.astype(BF)
    come = flipped(total, "mem", 1)
    reached = [jnp.concatenate([total, come], axis=0)]
    reached.append(flipped(reached[0], "mem", 3))
    g_own, sels, rts = [], [], []
    mats = None
    for r in range(8):
        res = pl.pallas_call(
            lambda *refs, r=r: own_kernel(r, *refs),
            out_shape=[sds((240, 1024), F32), sds((1152, 128), BF), sds((240, 256), BF)]
            + ([sds((480, 768), BF)] if r == 0 else []),
            in_specs=[VM] * 5,
            out_specs=[VM] * (4 if r == 0 else 3),
            scratch_shapes=[pltpu.VMEM((768, 1024), BF)],
            compiler_params=params(20),
            cost_estimate=cost(1.26e9, 3e6),
        )(pools[r], pair_col, pair_rot, rot_table, axial_shells if r == 0 else mats)
        if r == 0:
            mats = res[3]
        g_own.append(res[0])
        sels.append(res[1])
        rts.append(res[2])
    lifted = []
    for j in range(3):
        lifted.append(
            pl.pallas_call(
                lift_kernel,
                out_shape=sds((1920, 384), BF),
                in_specs=[VM] * 3,
                out_specs=VM,
                scratch_shapes=[pltpu.VMEM((240, 1024), BF)],
                compiler_params=params(20),
                cost_estimate=cost(0.7e9, 3e6),
            )(got[2 * j], got[2 * j + 1], axial_shells)
        )
    totals = []
    for q in range(4):
        totals.append(
            pl.pallas_call(
                recv_kernel,
                out_shape=sds((2, 240, 1024), F32),
                in_specs=[VM] * 7,
                out_specs=VM,
                compiler_params=params(20),
                cost_estimate=cost(1.2e9, 8e6),
            )(*lifted, sels[2 * q], sels[2 * q + 1], g_own[2 * q], g_own[2 * q + 1])
        )
    return pl.pallas_call(
        final_kernel,
        out_shape=sds((8, 240, 128), F32),
        in_specs=[VM] * 19,
        out_specs=VM,
        scratch_shapes=[
            pltpu.VMEM((2048, 1024), BF),
            pltpu.VMEM((512, 128), BF),
            pltpu.VMEM((8, 240, 128), F32),
        ],
        compiler_params=params(20),
        name="final",
    )(*totals, *rts, *reached, far_axial, cid, crot, incident, mie_coeffs)


def solution(mesh):
    in_specs = (
        P(None, None, ("grp", "mem")),
        P(None, None, ("grp", "mem")),
        P(),
        P(),
        P(),
        P(),
        P(),
        P(),
        P(("grp", "mem")),
        P(("grp", "mem")),
        P(None, ("grp", "mem")),
        P(None, ("grp", "mem")),
        P(("grp", "mem"), None),
    )
    out_specs = P(None, None, ("grp", "mem"))

    return jax.shard_map(
        on_device, mesh=mesh, in_specs=in_specs, out_specs=out_specs, check_vma=False
    )
```
